32 devices in a mesh: groups: 2 (over y), ctx: 16 (over z, x, core).
Axes of the slice: x: 2, y: 2, z: 4, core: 2. Of those that a mesh axis runs over, the one named last changes fastest.
Arguments:
- queries: bfloat16 [512, 5120], P(('groups', 'ctx')), parts along dimension 0, may hold values from -45 to 45
- keys: bfloat16 [49152, 1024], P(('groups', 'ctx')), parts along dimension 0, may hold values from -5 to 5
- values: bfloat16 [49152, 1024], P(('groups', 'ctx')), parts along dimension 0, may hold values from -10 to 10
- block_mask: int32 [16, 2, 192], P('groups', None, 'ctx'), parts along dimension 0, may hold values from 0 to 1, as said below
- out_weight: bfloat16 [5120, 5120], P('ctx'), may hold values from -0.078125 to 0.078125
Outputs:
- projected: bfloat16 [512, 5120], P(('groups', 'ctx')), parts along dimension 0
The draws below stay inside these ranges and needn't reach their ends.
There are 2 independent parts, one for each index of `groups`. The reference program is written for one: setup_inputs(seed, part) draws one part's arguments, and reference() takes and returns one part's arrays. A program takes and returns all parts, laid end to end along the dimension named above; an argument that names none is the same for every part. Nothing has to cross between parts.
Inputs may be any that keep to these rules, and one draw needn't show every extreme that they name: `block_mask`: for every key head and query block at least one key block is 1; the share of 1s differs between spans of 1536 positions.
All inputs are finite; a program needn't handle non-finite values.
Results may differ from the reference program's by a relative error of at most 0.0055.
Values may be sent and summed in bfloat16 or wider, within the bound.
A program may use at most 128 MiB of HBM per device.

```python
import math
import jax
import jax.numpy as jnp
from jax import lax

D = 5120
QUERY_HEADS = 40
KEY_VALUE_HEADS = 8
HEAD_SIZE = 128
MASK_BLOCK_SIZE = 128
QUERY_TOKENS = 256
KDEV = 1536
CACHED_POSITIONS = 24576


def forced_blocks(key):
    return jax.random.randint(jax.random.fold_in(key, 11), (KEY_VALUE_HEADS, QUERY_TOKENS // MASK_BLOCK_SIZE), 0, CACHED_POSITIONS // MASK_BLOCK_SIZE)


def shared_keys(key):
    base_random_key = jax.random.fold_in(key, 21)
    flattened_rows = jnp.clip(jax.random.normal(base_random_key, (CACHED_POSITIONS, KEY_VALUE_HEADS * HEAD_SIZE), jnp.float32), -5.0, 5.0)
    return flattened_rows


def draw_keys(key, part):
    flattened_rows = shared_keys(key)
    return flattened_rows.astype(jnp.bfloat16)


def draw_queries(key, part):
    query_key = jax.random.fold_in(key, 31)
    flattened_rows = jnp.clip(3.0 * jax.random.normal(query_key, (QUERY_TOKENS, D), jnp.float32), -18.0, 18.0)
    return flattened_rows.astype(jnp.bfloat16)


def draw_block_mask(key, part):
    query_block_count = QUERY_TOKENS // MASK_BLOCK_SIZE
    key_block_count = CACHED_POSITIONS // MASK_BLOCK_SIZE
    spans = CACHED_POSITIONS // KDEV
    share = jax.random.randint(jax.random.fold_in(key, 41), (spans,), 15, 56)
    share = jnp.repeat(share, KDEV // MASK_BLOCK_SIZE)
    random_rolls = jax.random.randint(jax.random.fold_in(key, 42), (KEY_VALUE_HEADS, query_block_count, key_block_count), 0, 100)
    live = random_rolls < share[None, None, :]
    forced = forced_blocks(key)
    hit = jnp.arange(key_block_count)[None, None, :] == forced[:, :, None]
    return (live | hit).astype(jnp.int32)


def level_of(stream_key, dims, pieces, smallest, largest):
    factor_of = 1.0
    for axis_at, parts in pieces:
        draws = jax.random.uniform(jax.random.fold_in(jax.random.fold_in(stream_key, 6), axis_at), (parts,), jnp.float32, smallest / len(pieces), largest / len(pieces))
        factor_of = factor_of * jnp.repeat(jnp.exp(draws), dims[axis_at] // parts).reshape((-1,) + (1,) * (len(dims) - 1 - axis_at))
    return factor_of


def normal_values(rng, extent, spread, limit, split=(), held_as=jnp.bfloat16):
    entries = spread * jax.random.normal(rng, extent, jnp.float32)
    if split:
        entries = entries * level_of(rng, extent, split, -0.22, 0.18)
    return jnp.clip(entries, -limit, limit).astype(held_as)


def setup_inputs(seed: int = 0, part: int = 0) -> dict:
    streams_of = jax.random.split(jax.random.key(seed), 6)
    part_splits = jax.random.split(jax.random.fold_in(streams_of[5], part), 6)
    return {
        "queries": draw_queries(jax.random.fold_in(jax.random.fold_in(streams_of[5], part), 71), part),
        "keys": draw_keys(jax.random.fold_in(jax.random.fold_in(streams_of[5], part), 71), part),
        "values": normal_values(part_splits[2], (CACHED_POSITIONS, KEY_VALUE_HEADS * HEAD_SIZE), 2.0, 10.0, ((0, 16),)),
        "block_mask": draw_block_mask(jax.random.fold_in(jax.random.fold_in(streams_of[5], part), 71), part),
        "out_weight": normal_values(streams_of[4], (D, D), D ** -0.5, 0.078125, ((0, 16),)),
    }


NEG = -1e+30

def reference(queries, keys, values, block_mask, out_weight):
    query_group = QUERY_HEADS // KEY_VALUE_HEADS
    scale = 1.0 / math.sqrt(HEAD_SIZE)
    q3 = queries.reshape(QUERY_TOKENS, QUERY_HEADS, HEAD_SIZE)
    key_tensor = keys.reshape(CACHED_POSITIONS, KEY_VALUE_HEADS, HEAD_SIZE)
    value_tensor = values.reshape(CACHED_POSITIONS, KEY_VALUE_HEADS, HEAD_SIZE)

    def one_head(head):
        kv_head = head // query_group
        q_h = lax.dynamic_index_in_dim(q3, head, 1, keepdims=False)
        k_h = lax.dynamic_index_in_dim(key_tensor, kv_head, 1, keepdims=False)
        v_h = lax.dynamic_index_in_dim(value_tensor, kv_head, 1, keepdims=False)
        scores = jnp.dot(q_h, k_h.T, preferred_element_type=jnp.float32) * scale
        blocks = lax.dynamic_index_in_dim(block_mask, kv_head, 0, keepdims=False)
        live = jnp.repeat(jnp.repeat(blocks > 0, MASK_BLOCK_SIZE, axis=0), MASK_BLOCK_SIZE, axis=1)
        top = lax.optimization_barrier(jnp.max(jnp.where(live, scores, NEG), axis=1, keepdims=True))
        probs = jnp.where(live, jnp.exp(scores - top), 0.0).astype(jnp.bfloat16)
        denom = lax.optimization_barrier(jnp.sum(probs.astype(jnp.float32), axis=1, keepdims=True))
        numer = jnp.dot(probs, v_h, preferred_element_type=jnp.float32)
        return numer / denom
    attn = lax.map(one_head, jnp.arange(QUERY_HEADS, dtype=jnp.int32))
    attn = jnp.transpose(attn, (1, 0, 2)).reshape(QUERY_TOKENS, D).astype(jnp.bfloat16)
    return jnp.dot(attn, out_weight, preferred_element_type=jnp.float32).astype(jnp.bfloat16)
```

```python
import functools
import math

import jax
import jax.numpy as jnp
from jax import lax
from jax.experimental import pallas as pl
from jax.experimental.pallas import tpu as pltpu
from jax.sharding import PartitionSpec as P

HEAD_SIZE = 128
NEG = -1e30
ONES = 16
LOG2E = math.log2(math.e)
MESH = pl.DeviceIdType.MESH
CORES, ROW = 2, 2


def attend_kernel(rows_each, mask_ref, q_ref, k_ref, v_ref, *refs):
    *numer_refs, top_ref, total_ref, live_ref, score_ref, query_ref, value_ref, sum_ref = refs
    head = pl.program_id(0)
    query_blocks, key_blocks = mask_ref.shape[1:]
    key_block = k_ref.shape[0] // key_blocks
    query_block = q_ref.shape[0] // query_blocks
    group = q_ref.shape[1] // HEAD_SIZE
    factor = LOG2E / math.sqrt(HEAD_SIZE)
    value_ref[:HEAD_SIZE] = v_ref[...].T
    value_ref[HEAD_SIZE:] = jnp.ones((ONES, v_ref.shape[0]), jnp.bfloat16)
    for at in range(query_blocks):
        rows = pl.ds(at * query_block, query_block)
        count = jnp.int32(0)
        for block in range(key_blocks):
            live_ref[count] = block
            count = count + (mask_ref[head, at, block] > 0).astype(jnp.int32)
        live_ref[count] = 0
        for g in range(group):
            tokens = q_ref[rows, g * HEAD_SIZE : (g + 1) * HEAD_SIZE]
            query_ref[:, g * query_block : (g + 1) * query_block] = tokens.T
        lanes = query_ref.shape[1]
        pairs = (count + 1) // 2

        def start_of(which):
            return pl.multiple_of(live_ref[which] * key_block, key_block)

        eights, quads = (count + 1) // 8, (count + 1) // 4

        def taken(ref_slice, first, blocks, axis):
            return jnp.concatenate([ref_slice(start_of(first + b)) for b in range(blocks)], axis=axis)

        def score_step(blocks, step, top):
            pair = step * (blocks // 2)
            keys = taken(lambda at: k_ref[pl.ds(at, key_block), :], 2 * pair, blocks, 0)
            scores = jnp.dot(keys, query_ref[...], preferred_element_type=jnp.float32)
            score_ref[pl.ds(pair, blocks // 2)] = scores.reshape(blocks // 2, 2 * key_block, lanes)
            tops = jnp.max(scores.reshape(blocks, key_block // 8, 8, lanes), axis=1)
            for b in range(blocks):
                one = tops[b]
                if b == blocks - 1:
                    one = jnp.where(2 * pair + b < count, one, NEG)
                top = jnp.maximum(top, one)
            return top

        top = jnp.full((8, lanes), NEG, jnp.float32)
        top = lax.fori_loop(0, eights, functools.partial(score_step, 8), top)
        top = lax.fori_loop(2 * eights, quads, functools.partial(score_step, 4), top)
        top = lax.fori_loop(2 * quads, pairs, functools.partial(score_step, 2), top)
        top = jnp.max(top, axis=0, keepdims=True) * factor
        sum_ref[...] = jnp.zeros_like(sum_ref)

        def sum_step(blocks, step, _):
            pair = step * (blocks // 2)
            probs = []
            for b in range(blocks):
                shift = top
                if b == blocks - 1:
                    shift = jnp.where(2 * pair + b < count, top, -NEG)
                half = slice(b % 2 * key_block, (b % 2 + 1) * key_block)
                scores = score_ref[pair + b // 2, half]
                probs.append(jnp.exp2(scores * factor - shift).astype(jnp.bfloat16))
            values = taken(lambda at: value_ref[:, pl.ds(at, key_block)], 2 * pair, blocks, 1)
            sum_ref[...] += jnp.dot(
                values, jnp.concatenate(probs, axis=0), preferred_element_type=jnp.float32
            )
            return 0

        lax.fori_loop(0, eights, functools.partial(sum_step, 8), 0)
        lax.fori_loop(2 * eights, quads, functools.partial(sum_step, 4), 0)
        lax.fori_loop(2 * quads, pairs, functools.partial(sum_step, 2), 0)
        numer = sum_ref[:HEAD_SIZE]
        top_ref[0, at : at + 1, :] = top
        total_ref[0, at : at + 1, :] = sum_ref[HEAD_SIZE : HEAD_SIZE + 1]
        for g in range(group):
            columns = slice(g * query_block, (g + 1) * query_block)
            out_columns = slice(g * HEAD_SIZE, (g + 1) * HEAD_SIZE)
            tokens = numer[:, columns].T
            if not rows_each:
                numer_refs[0][rows, out_columns] = tokens
                continue
            tokens = tokens.reshape(-1, CORES, rows_each, HEAD_SIZE)
            first = lax.rem(lax.axis_index("ctx"), CORES) == 0
            half = pl.ds(at * query_block // CORES, query_block // CORES)
            kept = jnp.where(first, tokens[:, 0], tokens[:, 1]).reshape(-1, HEAD_SIZE)
            sent = jnp.where(first, tokens[:, 1], tokens[:, 0]).reshape(-1, HEAD_SIZE)
            numer_refs[0][half, out_columns] = kept
            numer_refs[1][half, out_columns] = sent.astype(jnp.bfloat16)


def attend(whole, keys, values, block_mask, rows_each):
    qtok, width = whole.shape
    kdev = keys.shape[0]
    heads_kv, query_blocks, key_blocks = block_mask.shape
    columns = width // heads_kv
    lanes = columns // HEAD_SIZE * (qtok // query_blocks)
    stat = jax.ShapeDtypeStruct((heads_kv, query_blocks, lanes), jnp.float32)
    stat_spec = pl.BlockSpec((1, query_blocks, lanes), lambda h: (h, 0, 0))
    numers = [jax.ShapeDtypeStruct((qtok, width), jnp.float32)]
    if rows_each:
        numers = [jax.ShapeDtypeStruct((qtok // CORES, width), t) for t in (jnp.float32, jnp.bfloat16)]
    return pl.pallas_call(
        functools.partial(attend_kernel, rows_each),
        grid=(heads_kv,),
        out_shape=(*numers, stat, stat),
        in_specs=[
            pl.BlockSpec(memory_space=pltpu.SMEM),
            pl.BlockSpec((qtok, columns), lambda h: (0, h)),
            pl.BlockSpec((kdev, HEAD_SIZE), lambda h: (0, h)),
            pl.BlockSpec((kdev, HEAD_SIZE), lambda h: (0, h)),
        ],
        out_specs=(
            *(pl.BlockSpec((numer.shape[0], columns), lambda h: (0, h)) for numer in numers),
            stat_spec,
            stat_spec,
        ),
        scratch_shapes=[
            pltpu.SMEM((key_blocks + 2,), jnp.int32),
            pltpu.VMEM(((key_blocks + 1) // 2, 2 * kdev // key_blocks, lanes), jnp.float32),
            pltpu.VMEM((HEAD_SIZE, lanes), jnp.bfloat16),
            pltpu.VMEM((HEAD_SIZE + ONES, kdev), jnp.bfloat16),
            pltpu.VMEM((HEAD_SIZE + ONES, lanes), jnp.float32),
        ],
        compiler_params=pltpu.CompilerParams(vmem_limit_bytes=60 * 2**20),
        name="attend",
    )(block_mask, whole, keys, values)


def by_token(stat, qtok):
    heads_kv, query_blocks, _ = stat.shape
    stat = stat.reshape(heads_kv, query_blocks, -1, qtok // query_blocks)
    return stat.transpose(1, 3, 0, 2).reshape(qtok, -1)


def shards_any(queries, keys, values, block_mask, out_weight):
    whole = lax.all_gather(queries, "ctx", axis=0, tiled=True)
    qtok, width = whole.shape
    numer, top, total = attend(whole, keys, values, block_mask, 0)
    rescale = by_token(jnp.exp2(top - lax.pmax(top, "ctx")), qtok)
    denom = by_token(total, qtok) * rescale
    numer = (numer.reshape(qtok, -1, HEAD_SIZE) * rescale[:, :, None]).reshape(qtok, width)
    num_rows = lax.psum_scatter(numer, "ctx", scatter_dimension=0, tiled=True)
    den_rows = lax.psum_scatter(denom, "ctx", scatter_dimension=0, tiled=True)
    own_rows = num_rows.shape[0]
    attn_rows = (num_rows.reshape(own_rows, -1, HEAD_SIZE) / den_rows[:, :, None]).reshape(
        own_rows, width
    )
    attn_cols = lax.all_to_all(
        attn_rows.astype(jnp.bfloat16), "ctx", split_axis=1, concat_axis=0, tiled=True
    )
    summed = lax.psum_scatter(
        jnp.dot(attn_cols, out_weight, preferred_element_type=jnp.float32),
        "ctx",
        scatter_dimension=0,
        tiled=True,
    )
    return summed.astype(jnp.bfloat16)


def place(n):
    me = lax.axis_index("ctx")
    core = lax.rem(me, CORES)
    x = lax.rem(me // CORES, ROW)
    plane = me // (CORES * ROW)
    return me, plane, x, core


def index_of(plane, x, core):
    return (plane * ROW + x) * CORES + core


def remote(src, dst, send, recv, device):
    return pltpu.make_async_remote_copy(
        src_ref=src,
        dst_ref=dst,
        send_sem=send,
        recv_sem=recv,
        device_id={"ctx": device},
        device_id_type=MESH,
    )


LOW = -1e28
LANES = 128
SIDES = 2


def swap_halves(stat):
    return pltpu.roll(stat, LANES // 2, 1)


def weigh(stats):
    lane = lax.broadcasted_iota(jnp.int32, stats[0].shape, 1)
    top = functools.reduce(jnp.maximum, stats)
    factors = [jnp.exp2(stat - top) for stat in stats]
    total = sum(stat * swap_halves(factor) for stat, factor in zip(stats, factors))
    return factors, jnp.where(lane < LANES // 2, top, total)


def column(tile, first, g, group):
    lanes = [first + half * group + g for half in range(2)]
    return jnp.concatenate([tile[:, lane : lane + 1] for lane in lanes], axis=0)


def layer_kernel(
    shape,
    own_ref,
    k_hbm,
    v_hbm,
    mask_ref,
    w_hbm,
    out_ref,
    whole,
    k_ref,
    v_ref,
    w_ref,
    score0,
    score1,
    top0,
    top1,
    local_sem,
    gather_sem,
    gather_plane_sem,
    kept,
    sent,
    core_in,
    beside_out,
    mine,
    beside_in,
    plane_out,
    own,
    plane_in,
    stat,
    stat_core_in,
    stat_mine,
    stat_beside_in,
    stat_merged,
    stat_plane_in,
    sum_sem,
    sum_plane_sem,
    pieces,
    columns_ref,
    swap_sem,
    p_kept,
    p_sent,
    p_core_in,
    p_beside_out,
    p_mine,
    p_beside_in,
    p_plane_out,
    p_own,
    p_plane_in,
    p_sem,
    p_plane_sem,
):
    n, planes, heads, group, query_block, key_blocks, key_block = shape
    me, plane, x, core = place(n)
    beside, sibling = 1 - x, 1 - core
    rows = own_ref.shape[0]
    span = planes // SIDES
    wide = group * HEAD_SIZE
    share = wide // 2
    factor = LOG2E / math.sqrt(HEAD_SIZE)
    slots = 8
    to_beside = index_of(plane, beside, core)
    to_sibling = index_of(plane, x, sibling)
    others = [lax.rem(plane + step, planes) for step in range(1, planes)]

    def at_head(h, width=wide):
        return pl.ds(pl.multiple_of(h * width, width), width)

    keys_in = pltpu.make_async_copy(k_hbm, k_ref, local_sem.at[0])
    values_in = pltpu.make_async_copy(v_hbm, v_ref, local_sem.at[1])
    weight_in = pltpu.make_async_copy(w_hbm, w_ref, local_sem.at[2])
    own_in = pltpu.make_async_copy(own_ref, whole.at[plane, x, core], local_sem.at[3])
    own_in.start()
    keys_in.start()
    values_in.start()
    weight_in.start()
    barrier = pltpu.get_barrier_semaphore()
    for step in range(1, n):
        pl.semaphore_signal(
            barrier, inc=1, device_id={"ctx": lax.rem(me + step, n)}, device_id_type=MESH
        )
    pl.semaphore_wait(barrier, n - 1)
    own_in.wait()

    def gather_plane(h, p, source):
        block = whole.at[source, x, core, :, at_head(h)]
        return remote(
            block,
            block,
            gather_plane_sem.at[0, h, p],
            gather_plane_sem.at[1, h, source],
            index_of(p, x, core),
        )

    def gather_beside(h, side):
        block = whole.at[:, side, core, :, at_head(h)]
        return remote(block, block, gather_sem.at[0, h], gather_sem.at[1, h], to_beside)

    def gather_sibling(h, which):
        block = whole.at[:, :, which, :, at_head(h)]
        return remote(block, block, gather_sem.at[2, h], gather_sem.at[3, h], to_sibling)

    def gather0(h):
        for p in others:
            gather_plane(h, p, plane).start()

    def gather1(h):
        for p in others:
            gather_plane(h, p, p).wait_recv()
        gather_beside(h, x).start()

    def gather2(h):
        gather_beside(h, beside).wait_recv()
        gather_sibling(h, core).start()

    def gather3(h):
        gather_sibling(h, sibling).wait_recv()

    def score_item(h, t, score, top_ref):
        tokens = whole.at[t * span : (t + 1) * span]
        query = jnp.concatenate(
            [
                tokens[:, :, :, :, pl.ds(pl.multiple_of(h * wide + g * HEAD_SIZE, HEAD_SIZE), HEAD_SIZE)].reshape(
                    query_block, HEAD_SIZE
                )
                for g in range(group)
            ],
            axis=0,
        )
        top = None
        for pair in range(key_blocks // 2):
            at = slice(2 * pair * key_block, 2 * (pair + 1) * key_block)
            scores = lax.dot_general(
                query,
                k_ref[at, at_head(h, HEAD_SIZE)],
                (((1,), (1,)), ((), ())),
                preferred_element_type=jnp.float32,
            )
            for b in range(2):
                block = 2 * pair + b
                bias = jnp.where(mask_ref[h, t, block] > 0, 0.0, NEG)
                part = scores[:, b * key_block : (b + 1) * key_block] + bias
                score[:, block * key_block : (block + 1) * key_block] = part
                top = part if top is None else jnp.maximum(top, part)
        top = jnp.maximum(jnp.max(top, axis=1, keepdims=True) * factor, LOW)
        top_ref[...] = jnp.broadcast_to(top, top_ref.shape)

    def sum_item(h, t, score, top_ref):
        top = top_ref[...]
        shift = jnp.concatenate([top, top], axis=1)
        both = None
        for pair in range(key_blocks // 2):
            at = slice(2 * pair * key_block, 2 * (pair + 1) * key_block)
            probs = jnp.exp2(score[:, at] * factor - shift).astype(jnp.bfloat16)
            values = jnp.concatenate(
                [
                    v_ref[at, at_head(h, HEAD_SIZE)],
                    jnp.ones((2 * key_block, HEAD_SIZE), jnp.bfloat16),
                ],
                axis=1,
            )
            part = jnp.dot(probs, values, preferred_element_type=jnp.float32)
            both = part if both is None else both + part
        split = (group, span, ROW, CORES, rows, HEAD_SIZE)
        numer = both[:, :HEAD_SIZE].reshape(split)
        total = both[:, HEAD_SIZE:].reshape(split)
        tops = top.reshape(split)
        for g in range(group):
            at = slice(g * HEAD_SIZE, (g + 1) * HEAD_SIZE)
            one, two = numer[g, :, :, 0], numer[g, :, :, 1]
            kept[h, t, :, :, :, at] = jnp.where(core == 0, one, two)
            sent[h, t, :, :, :, at] = jnp.where(core == 0, two, one).astype(jnp.bfloat16)
        lane = lax.broadcasted_iota(jnp.int32, (8, LANES), 1)
        for which in range(CORES):
            for side in range(ROW):
                tile = jnp.zeros((8, LANES), jnp.float32)
                for q in range(span):
                    for half in range(rows // 8):
                        at = slice(half * 8, half * 8 + 8)
                        for g in range(group):
                            to = (q * 2 + half) * slots + g
                            tile = jnp.where(lane == to, tops[g, q, side, which, at], tile)
                            to = to + LANES // 2
                            tile = jnp.where(lane == to, total[g, q, side, which, at], tile)
                stat[h, t, which, side] = tile

    def to_core(h, t):
        return [
            remote(sent.at[h, t], core_in.at[h, t], sum_sem.at[0, h, t], sum_sem.at[1, h, t], to_sibling),
            remote(
                stat.at[h, t, sibling],
                stat_core_in.at[h, t],
                sum_sem.at[2, h, t],
                sum_sem.at[3, h, t],
                to_sibling,
            ),
        ]

    def to_side(h, t):
        return [
            remote(
                beside_out.at[h, t],
                beside_in.at[h, t],
                sum_sem.at[4, h, t],
                sum_sem.at[5, h, t],
                to_beside,
            ),
            remote(
                stat_mine.at[h, t, beside],
                stat_beside_in.at[h, t],
                sum_sem.at[6, h, t],
                sum_sem.at[7, h, t],
                to_beside,
            ),
        ]

    def to_plane(h, t, p, slot):
        device = index_of(p, x, core)
        return [
            remote(
                plane_out.at[h, p],
                plane_in.at[h, slot],
                sum_plane_sem.at[0, h, p],
                sum_plane_sem.at[1, h, slot],
                device,
            ),
            remote(
                stat_merged.at[h, t],
                stat_plane_in.at[h, slot],
                sum_plane_sem.at[2, h, p],
                sum_plane_sem.at[3, h, slot],
                device,
            ),
        ]

    def start(copies):
        for copy in copies:
            copy.start()

    def arrive(copies):
        for copy in copies:
            copy.wait_recv()

    def leave(copies):
        for copy in copies:
            copy.wait_send()

    def sum0(h, t):
        start(to_core(h, t))

    def sum1(h, t):
        arrive(to_core(h, t))
        for out in (0, 1):
            side = beside if out == 0 else x
            factors, merged = weigh([stat[h, t, core, side], stat_core_in[h, t, side]])
            stat_mine[h, t, side] = merged
            for q in range(span):
                for g in range(group):
                    at = slice(g * HEAD_SIZE, (g + 1) * HEAD_SIZE)
                    one, two = [column(one, q * 2 * slots, g, slots) for one in factors]
                    value = (
                        kept[h, t, q, side, :, at] * one
                        + core_in[h, t, q, side, :, at].astype(jnp.float32) * two
                    )
                    if out == 0:
                        beside_out[h, t, q, :, at] = value.astype(jnp.bfloat16)
                    else:
                        mine[h, t, q, :, at] = value
            if out == 0:
                start(to_side(h, t))

    def sum2(h, t):
        arrive(to_side(h, t))
        factors, merged = weigh([stat_mine[h, t, x], stat_beside_in[h, t]])
        stat_merged[h, t] = merged
        for q in range(span):
            p = t * span + q
            values = []
            for g in range(group):
                at = slice(g * HEAD_SIZE, (g + 1) * HEAD_SIZE)
                one, two = [column(one, q * 2 * slots, g, slots) for one in factors]
                values.append(
                    mine[h, t, q, :, at] * one + beside_in[h, t, q, :, at].astype(jnp.float32) * two
                )
            value = jnp.concatenate(values, axis=1)

            @pl.when(plane == p)
            def _():
                own[h] = value

            @pl.when(plane != p)
            def _():
                plane_out[h, p] = value.astype(jnp.bfloat16)
                start(to_plane(h, t, p, plane))

    def swap(device, h, j, slot):
        return remote(
            pieces.at[h, j], columns_ref.at[slot], swap_sem.at[0, device], swap_sem.at[1, slot], device
        )

    def keep_piece(h, j):
        return pltpu.make_async_copy(pieces.at[h, j], columns_ref.at[me], local_sem.at[4])

    def sum3(h):
        for p in others:
            arrive(to_plane(h, 0, p, p))
        tiles = [stat_merged[h, plane // span]] + [stat_plane_in[h, p] for p in others]
        odd = lax.rem(plane, span) == 1
        tiles = [jnp.where(odd, pltpu.roll(tile, LANES - 2 * slots, 1), tile) for tile in tiles]
        factors, merged = weigh(tiles)
        merged = swap_halves(merged)
        for g in range(group):
            at = slice(g * HEAD_SIZE, (g + 1) * HEAD_SIZE)
            value = own[h, :, at] * column(factors[0], 0, g, slots)
            for p, one in zip(others, factors[1:]):
                value = value + plane_in[h, p, :, at].astype(jnp.float32) * column(one, 0, g, slots)
            value = (value / column(merged, 0, g, slots)).astype(jnp.bfloat16)
            low, high = g * HEAD_SIZE, (g + 1) * HEAD_SIZE
            for j in range(2):
                first, last = max(low, j * share), min(high, (j + 1) * share)
                if first < last:
                    pieces[h, j, :, first - j * share : last - j * share] = value[:, first - low : last - low]
        for j in range(2):
            device = 2 * h + j

            @pl.when(device == me)
            def _():
                keep_piece(h, j).start()

            @pl.when(device != me)
            def _():
                swap(device, h, j, me).start()

    def between(h, t):
        def on(cond, act):
            pl.when(cond)(act)

        if t == 0:
            on(h >= 1, lambda: sum0(h - 1, 1))
            on(h + 5 < heads, lambda: gather0(h + 5))
            on(h + 3 < heads, lambda: gather1(h + 3))
            on(h >= 1, lambda: sum1(h - 1, 0))
            on(h >= 3, lambda: sum2(h - 3, 1))
        else:
            sum0(h, 0)
            on(h + 2 < heads, lambda: gather2(h + 2))
            on(h + 1 < heads, lambda: gather3(h + 1))
            on(h >= 1, lambda: sum1(h - 1, 1))
            on(h >= 2, lambda: sum2(h - 2, 0))
            on(h >= 4, lambda: sum3(h - 4))

    gather0(0)
    gather0(1)
    gather0(2)
    gather1(0)
    gather0(3)
    gather1(1)
    gather2(0)
    gather0(4)
    gather1(2)
    gather2(1)
    keys_in.wait()
    values_in.wait()
    gather3(0)
    score_item(0, 0, score0, top0)

    def head_step(h, _):
        between(h, 0)
        score_item(h, 1, score1, top1)
        sum_item(h, 0, score0, top0)
        between(h, 1)
        score_item(jnp.minimum(h + 1, heads - 1), 0, score0, top0)
        sum_item(h, 1, score1, top1)
        return 0

    lax.fori_loop(0, heads, head_step, 0)
    last = heads - 1
    sum0(last, 1)
    sum1(last, 0)
    sum2(last - 2, 1)
    sum1(last, 1)
    sum2(last - 1, 0)
    sum2(last - 1, 1)
    sum2(last, 0)
    sum2(last, 1)

    def finish_head(h, _):
        sum3(h)
        return 0

    lax.fori_loop(heads - 4, heads, finish_head, 0)
    weight_in.wait()

    def take_piece(step, _):
        device = lax.rem(me + step, n)
        swap(device, 0, 0, device).wait_recv()
        return 0

    lax.fori_loop(1, n, take_piece, 0)
    keep_piece(0, 0).wait()

    tiles = out_ref.shape[1] // wide

    def p_core(c):
        return remote(p_sent.at[c], p_core_in.at[c], p_sem.at[0, c], p_sem.at[1, c], to_sibling)

    def p_side(c):
        return remote(p_beside_out.at[c], p_beside_in.at[c], p_sem.at[2, c], p_sem.at[3, c], to_beside)

    def p_plane(c, p, slot):
        return remote(
            p_plane_out.at[c, p],
            p_plane_in.at[c, slot],
            p_plane_sem.at[0, c, p],
            p_plane_sem.at[1, c, slot],
            index_of(p, x, core),
        )

    def project0(c):
        cols = columns_ref[...].reshape(n * rows, share)
        product = jnp.dot(cols, w_ref[:, at_head(c)], preferred_element_type=jnp.float32)
        product = product.reshape(planes, ROW, CORES, rows, wide)
        one, two = product[:, :, 0], product[:, :, 1]
        p_sent[c] = jnp.where(core == 0, two, one).astype(jnp.bfloat16)
        p_core(c).start()
        p_kept[c] = jnp.where(core == 0, one, two)

    def project1(c):
        p_core(c).wait_recv()
        p_beside_out[c] = (
            p_kept[c, :, beside] + p_core_in[c, :, beside].astype(jnp.float32)
        ).astype(jnp.bfloat16)
        p_side(c).start()
        p_mine[c] = p_kept[c, :, x] + p_core_in[c, :, x].astype(jnp.float32)

    def project2(c):
        p_side(c).wait_recv()
        for p in others:
            value = p_mine[c, p] + p_beside_in[c, p].astype(jnp.float32)
            p_plane_out[c, p] = value.astype(jnp.bfloat16)
            p_plane(c, p, plane).start()
        p_own[c] = p_mine[c, plane] + p_beside_in[c, plane].astype(jnp.float32)

    def project3(c):
        for p in others:
            p_plane(c, p, p).wait_recv()
        value = p_own[c]
        for p in others:
            value = value + p_plane_in[c, p].astype(jnp.float32)
        out_ref[:, at_head(c)] = value.astype(out_ref.dtype)

    def product_step(c, _):
        pl.when(c < tiles)(lambda: project0(c))
        pl.when(c >= 1)(lambda: project1(c - 1))
        return 0

    def second_step(c, _):
        project2(c)
        return 0

    def third_step(c, _):
        project3(c)
        return 0

    lax.fori_loop(0, tiles + 1, product_step, 0)
    lax.fori_loop(0, tiles, second_step, 0)
    lax.fori_loop(0, tiles, third_step, 0)

    def drain(h, _):
        for p in others:
            gather_plane(h, p, plane).wait_send()
            p_plane(h, p, plane).wait_send()
        gather_beside(h, x).wait_send()
        gather_sibling(h, core).wait_send()
        p_core(h).wait_send()
        p_side(h).wait_send()
        for t in range(SIDES):
            leave(to_core(h, t))
            leave(to_side(h, t))
        for p in range(planes):

            @pl.when(plane != p)
            def _():
                leave(to_plane(h, p // span, p, plane))

        for j in range(2):
            device = 2 * h + j

            @pl.when(device != me)
            def _():
                swap(device, h, j, me).wait_send()

        return 0

    lax.fori_loop(0, heads, drain, 0)


def layer(queries, keys, values, block_mask, weight, n):
    rows, width = queries.shape
    heads, query_blocks, key_blocks = block_mask.shape
    kdev = keys.shape[0]
    planes = n // (CORES * ROW)
    wide = width // heads
    group = wide // HEAD_SIZE
    query_block = n * rows // query_blocks
    span = planes // query_blocks
    items = (heads, query_blocks)
    bf16, f32 = jnp.bfloat16, jnp.float32
    dma = pltpu.SemaphoreType.DMA

    def reduce_scratch(lead, across, middle):
        return [
            pltpu.VMEM((*lead, across, ROW, rows, wide), f32),
            pltpu.VMEM((*lead, across, ROW, rows, wide), bf16),
            pltpu.VMEM((*lead, across, ROW, rows, wide), bf16),
            pltpu.VMEM((*lead, across, rows, wide), bf16),
            pltpu.VMEM((*lead, across, rows, wide), f32),
            pltpu.VMEM((*lead, across, rows, wide), bf16),
            pltpu.VMEM((heads, planes, rows, wide), bf16),
            pltpu.VMEM((heads, rows, wide), f32),
            pltpu.VMEM((heads, planes, rows, wide), bf16),
        ]

    lanes = group * query_block
    shape = (n, planes, heads, group, query_block, key_blocks, kdev // key_blocks)
    return pl.pallas_call(
        functools.partial(layer_kernel, shape),
        out_shape=jax.ShapeDtypeStruct((rows, width), bf16),
        in_specs=[
            pl.BlockSpec(memory_space=pltpu.VMEM),
            pl.BlockSpec(memory_space=pl.ANY),
            pl.BlockSpec(memory_space=pl.ANY),
            pl.BlockSpec(memory_space=pltpu.SMEM),
            pl.BlockSpec(memory_space=pl.ANY),
        ],
        out_specs=pl.BlockSpec(memory_space=pltpu.VMEM),
        scratch_shapes=[
            pltpu.VMEM((planes, ROW, CORES, rows, width), bf16),
            pltpu.VMEM(keys.shape, bf16),
            pltpu.VMEM(values.shape, bf16),
            pltpu.VMEM(weight.shape, bf16),
            pltpu.VMEM((lanes, kdev), f32),
            pltpu.VMEM((lanes, kdev), f32),
            pltpu.VMEM((lanes, LANES), f32),
            pltpu.VMEM((lanes, LANES), f32),
            dma((5,)),
            dma((4, heads)),
            dma((2, heads, planes)),
            *reduce_scratch(items, span, None),
            pltpu.VMEM((*items, CORES, ROW, 8, LANES), f32),
            pltpu.VMEM((*items, ROW, 8, LANES), f32),
            pltpu.VMEM((*items, ROW, 8, LANES), f32),
            pltpu.VMEM((*items, 8, LANES), f32),
            pltpu.VMEM((*items, 8, LANES), f32),
            pltpu.VMEM((heads, planes, 8, LANES), f32),
            dma((8, *items)),
            dma((4, heads, planes)),
            pltpu.VMEM((heads, 2, rows, wide // 2), bf16),
            pltpu.VMEM((n, rows, wide // 2), bf16),
            dma((2, n)),
            *reduce_scratch((heads,), planes, None),
            dma((4, heads)),
            dma((2, heads, planes)),
        ],
        compiler_params=pltpu.CompilerParams(
            collective_id=0, has_side_effects=True, vmem_limit_bytes=60 * 2**20
        ),
        name="layer",
    )(queries, keys, values, block_mask, weight)


def solution(mesh):
    n = mesh.shape["ctx"]

    def shards(queries, keys, values, block_mask, out_weight):
        rows, width = queries.shape
        heads, query_blocks, key_blocks = block_mask.shape
        planes = n // (CORES * ROW)
        group = width // heads // HEAD_SIZE
        fits = (
            n == CORES * ROW * planes
            and n == 2 * heads
            and rows == 16
            and query_blocks == SIDES
            and planes == 2 * SIDES
            and group <= 8
            and key_blocks % 2 == 0
        )
        if fits:
            return layer(queries, keys, values, block_mask, out_weight, n)
        return shards_any(queries, keys, values, block_mask, out_weight)

    return jax.shard_map(
        shards,
        mesh=mesh,
        in_specs=(
            P(("groups", "ctx"), None),
            P(("groups", "ctx"), None),
            P(("groups", "ctx"), None),
            P("groups", None, "ctx"),
            P("ctx", None),
        ),
        out_specs=P(("groups", "ctx"), None),
        check_vma=False,
    )
```

```python
import functools
import math

import jax
import jax.numpy as jnp
from jax import lax
from jax.experimental import pallas as pl
from jax.experimental.pallas import tpu as pltpu
from jax.sharding import PartitionSpec as P

HEAD_SIZE = 128
NEG = -1e30
ONES = 16
LOG2E = math.log2(math.e)
MESH = pl.DeviceIdType.MESH
CORES, ROW = 2, 2


def attend_kernel(rows_each, mask_ref, q_ref, k_ref, v_ref, *refs):
    *numer_refs, top_ref, total_ref, live_ref, score_ref, query_ref, value_ref, sum_ref = refs
    head = pl.program_id(0)
    query_blocks, key_blocks = mask_ref.shape[1:]
    key_block = k_ref.shape[0] // key_blocks
    query_block = q_ref.shape[0] // query_blocks
    group = q_ref.shape[1] // HEAD_SIZE
    factor = LOG2E / math.sqrt(HEAD_SIZE)
    value_ref[:HEAD_SIZE] = v_ref[...].T
    value_ref[HEAD_SIZE:] = jnp.ones((ONES, v_ref.shape[0]), jnp.bfloat16)
    for at in range(query_blocks):
        rows = pl.ds(at * query_block, query_block)
        count = jnp.int32(0)
        for block in range(key_blocks):
            live_ref[count] = block
            count = count + (mask_ref[head, at, block] > 0).astype(jnp.int32)
        live_ref[count] = 0
        for g in range(group):
            tokens = q_ref[rows, g * HEAD_SIZE : (g + 1) * HEAD_SIZE]
            query_ref[:, g * query_block : (g + 1) * query_block] = tokens.T
        lanes = query_ref.shape[1]
        pairs = (count + 1) // 2

        def start_of(which):
            return pl.multiple_of(live_ref[which] * key_block, key_block)

        eights, quads = (count + 1) // 8, (count + 1) // 4

        def taken(ref_slice, first, blocks, axis):
            return jnp.concatenate([ref_slice(start_of(first + b)) for b in range(blocks)], axis=axis)

        def score_step(blocks, step, top):
            pair = step * (blocks // 2)
            keys = taken(lambda at: k_ref[pl.ds(at, key_block), :], 2 * pair, blocks, 0)
            scores = jnp.dot(keys, query_ref[...], preferred_element_type=jnp.float32)
            score_ref[pl.ds(pair, blocks // 2)] = scores.reshape(blocks // 2, 2 * key_block, lanes)
            tops = jnp.max(scores.reshape(blocks, key_block // 8, 8, lanes), axis=1)
            for b in range(blocks):
                one = tops[b]
                if b == blocks - 1:
                    one = jnp.where(2 * pair + b < count, one, NEG)
                top = jnp.maximum(top, one)
            return top

        top = jnp.full((8, lanes), NEG, jnp.float32)
        top = lax.fori_loop(0, eights, functools.partial(score_step, 8), top)
        top = lax.fori_loop(2 * eights, quads, functools.partial(score_step, 4), top)
        top = lax.fori_loop(2 * quads, pairs, functools.partial(score_step, 2), top)
        top = jnp.max(top, axis=0, keepdims=True) * factor
        sum_ref[...] = jnp.zeros_like(sum_ref)

        def sum_step(blocks, step, _):
            pair = step * (blocks // 2)
            probs = []
            for b in range(blocks):
                shift = top
                if b == blocks - 1:
                    shift = jnp.where(2 * pair + b < count, top, -NEG)
                half = slice(b % 2 * key_block, (b % 2 + 1) * key_block)
                scores = score_ref[pair + b // 2, half]
                probs.append(jnp.exp2(scores * factor - shift).astype(jnp.bfloat16))
            values = taken(lambda at: value_ref[:, pl.ds(at, key_block)], 2 * pair, blocks, 1)
            sum_ref[...] += jnp.dot(
                values, jnp.concatenate(probs, axis=0), preferred_element_type=jnp.float32
            )
            return 0

        lax.fori_loop(0, eights, functools.partial(sum_step, 8), 0)
        lax.fori_loop(2 * eights, quads, functools.partial(sum_step, 4), 0)
        lax.fori_loop(2 * quads, pairs, functools.partial(sum_step, 2), 0)
        numer = sum_ref[:HEAD_SIZE]
        top_ref[0, at : at + 1, :] = top
        total_ref[0, at : at + 1, :] = sum_ref[HEAD_SIZE : HEAD_SIZE + 1]
        for g in range(group):
            columns = slice(g * query_block, (g + 1) * query_block)
            out_columns = slice(g * HEAD_SIZE, (g + 1) * HEAD_SIZE)
            tokens = numer[:, columns].T
            if not rows_each:
                numer_refs[0][rows, out_columns] = tokens
                continue
            tokens = tokens.reshape(-1, CORES, rows_each, HEAD_SIZE)
            first = lax.rem(lax.axis_index("ctx"), CORES) == 0
            half = pl.ds(at * query_block // CORES, query_block // CORES)
            kept = jnp.where(first, tokens[:, 0], tokens[:, 1]).reshape(-1, HEAD_SIZE)
            sent = jnp.where(first, tokens[:, 1], tokens[:, 0]).reshape(-1, HEAD_SIZE)
            numer_refs[0][half, out_columns] = kept
            numer_refs[1][half, out_columns] = sent.astype(jnp.bfloat16)


def attend(whole, keys, values, block_mask, rows_each):
    qtok, width = whole.shape
    kdev = keys.shape[0]
    heads_kv, query_blocks, key_blocks = block_mask.shape
    columns = width // heads_kv
    lanes = columns // HEAD_SIZE * (qtok // query_blocks)
    stat = jax.ShapeDtypeStruct((heads_kv, query_blocks, lanes), jnp.float32)
    stat_spec = pl.BlockSpec((1, query_blocks, lanes), lambda h: (h, 0, 0))
    numers = [jax.ShapeDtypeStruct((qtok, width), jnp.float32)]
    if rows_each:
        numers = [jax.ShapeDtypeStruct((qtok // CORES, width), t) for t in (jnp.float32, jnp.bfloat16)]
    return pl.pallas_call(
        functools.partial(attend_kernel, rows_each),
        grid=(heads_kv,),
        out_shape=(*numers, stat, stat),
        in_specs=[
            pl.BlockSpec(memory_space=pltpu.SMEM),
            pl.BlockSpec((qtok, columns), lambda h: (0, h)),
            pl.BlockSpec((kdev, HEAD_SIZE), lambda h: (0, h)),
            pl.BlockSpec((kdev, HEAD_SIZE), lambda h: (0, h)),
        ],
        out_specs=(
            *(pl.BlockSpec((numer.shape[0], columns), lambda h: (0, h)) for numer in numers),
            stat_spec,
            stat_spec,
        ),
        scratch_shapes=[
            pltpu.SMEM((key_blocks + 2,), jnp.int32),
            pltpu.VMEM(((key_blocks + 1) // 2, 2 * kdev // key_blocks, lanes), jnp.float32),
            pltpu.VMEM((HEAD_SIZE, lanes), jnp.bfloat16),
            pltpu.VMEM((HEAD_SIZE + ONES, kdev), jnp.bfloat16),
            pltpu.VMEM((HEAD_SIZE + ONES, lanes), jnp.float32),
        ],
        compiler_params=pltpu.CompilerParams(vmem_limit_bytes=60 * 2**20),
        name="attend",
    )(block_mask, whole, keys, values)


def by_token(stat, qtok):
    heads_kv, query_blocks, _ = stat.shape
    stat = stat.reshape(heads_kv, query_blocks, -1, qtok // query_blocks)
    return stat.transpose(1, 3, 0, 2).reshape(qtok, -1)


def shards_any(queries, keys, values, block_mask, out_weight):
    whole = lax.all_gather(queries, "ctx", axis=0, tiled=True)
    qtok, width = whole.shape
    numer, top, total = attend(whole, keys, values, block_mask, 0)
    rescale = by_token(jnp.exp2(top - lax.pmax(top, "ctx")), qtok)
    denom = by_token(total, qtok) * rescale
    numer = (numer.reshape(qtok, -1, HEAD_SIZE) * rescale[:, :, None]).reshape(qtok, width)
    num_rows = lax.psum_scatter(numer, "ctx", scatter_dimension=0, tiled=True)
    den_rows = lax.psum_scatter(denom, "ctx", scatter_dimension=0, tiled=True)
    own_rows = num_rows.shape[0]
    attn_rows = (num_rows.reshape(own_rows, -1, HEAD_SIZE) / den_rows[:, :, None]).reshape(
        own_rows, width
    )
    attn_cols = lax.all_to_all(
        attn_rows.astype(jnp.bfloat16), "ctx", split_axis=1, concat_axis=0, tiled=True
    )
    summed = lax.psum_scatter(
        jnp.dot(attn_cols, out_weight, preferred_element_type=jnp.float32),
        "ctx",
        scatter_dimension=0,
        tiled=True,
    )
    return summed.astype(jnp.bfloat16)


def place(n):
    me = lax.axis_index("ctx")
    core = lax.rem(me, CORES)
    x = lax.rem(me // CORES, ROW)
    plane = me // (CORES * ROW)
    return me, plane, x, core


def index_of(plane, x, core):
    return (plane * ROW + x) * CORES + core


def remote(src, dst, send, recv, device):
    return pltpu.make_async_remote_copy(
        src_ref=src,
        dst_ref=dst,
        send_sem=send,
        recv_sem=recv,
        device_id={"ctx": device},
        device_id_type=MESH,
    )


LOW = -1e28
LANES = 128
SIDES = 2
TILE = 256


def swap_halves(stat):
    return pltpu.roll(stat, LANES // 2, 1)


def weigh(stats):
    lane = lax.broadcasted_iota(jnp.int32, stats[0].shape, 1)
    top = functools.reduce(jnp.maximum, stats)
    factors = [jnp.exp2(stat - top) for stat in stats]
    total = sum(stat * swap_halves(factor) for stat, factor in zip(stats, factors))
    return factors, jnp.where(lane < LANES // 2, top, total)


def column(tile, first, g, slots):
    lanes = [first + half * slots + g for half in range(2)]
    return jnp.concatenate([tile[:, lane : lane + 1] for lane in lanes], axis=0)


def layer_kernel(
    shape,
    own_hbm,
    k_hbm,
    v_hbm,
    mask_ref,
    w_hbm,
    out_ref,
    whole,
    k_ref,
    v_ref,
    w_ref,
    bias_ref,
    bias_out,
    score0,
    score1,
    top0,
    top1,
    local_sem,
    kv_sem,
    gather_sem,
    gather_plane_sem,
    beside_out,
    mine,
    beside_in,
    plane_out,
    own,
    plane_in,
    stat,
    stat_beside_in,
    stat_merged,
    stat_plane_in,
    sum_sem,
    sum_plane_sem,
    pieces,
    columns_ref,
    swap_sem,
    p_out,
    p_mine,
    p_in,
    p_plane_out,
    p_own,
    p_plane_in,
    p_last,
    p_sem,
    p_plane_sem,
):
    n, planes, heads, group, query_block, key_blocks, key_block = shape
    me, plane, x, core = place(n)
    beside, sibling = 1 - x, 1 - core
    rows = own_hbm.shape[0]
    span = planes // SIDES
    wide = group * HEAD_SIZE
    each = heads // CORES
    factor = LOG2E / math.sqrt(HEAD_SIZE)
    slots = 8
    pair, odd = plane // span, lax.rem(plane, span)
    near = pair * span + 1 - odd
    other = 1 - pair
    away = [other * span + odd, other * span + 1 - odd]
    others = [near] + away
    to_beside = index_of(plane, beside, core)
    to_sibling = index_of(plane, x, sibling)

    def lanes_at(start, width, unit=LANES):
        return pl.ds(pl.multiple_of(start, unit), width)

    def at_head(j):
        return lanes_at(j * wide, wide)

    half_width = each * wide
    queries_in = pltpu.make_async_copy(
        own_hbm.at[:, lanes_at(core * half_width, half_width)], whole.at[plane, x, core], local_sem.at[0]
    )
    queries_in.start()

    def kv_local(which, hbm, ref, j):
        return pltpu.make_async_copy(
            hbm.at[:, lanes_at((core * each + j) * HEAD_SIZE, HEAD_SIZE)],
            ref.at[core, :, lanes_at(j * HEAD_SIZE, HEAD_SIZE)],
            kv_sem.at[which, j],
        )

    def kv_remote(which, hbm, ref, j, source):
        return remote(
            hbm.at[:, lanes_at((sibling * each + j) * HEAD_SIZE, HEAD_SIZE)],
            ref.at[source, :, lanes_at(j * HEAD_SIZE, HEAD_SIZE)],
            kv_sem.at[2 + which, j],
            kv_sem.at[4 + which, j],
            to_sibling,
        )

    kv = [(0, k_hbm, k_ref), (1, v_hbm, v_ref)]
    w_local = pltpu.make_async_copy(
        w_hbm.at[:, lanes_at(core * half_width, half_width)], w_ref.at[core], local_sem.at[1]
    )

    def w_remote(source):
        return remote(
            w_hbm.at[:, lanes_at(sibling * half_width, half_width)],
            w_ref.at[source],
            local_sem.at[2],
            local_sem.at[3],
            to_sibling,
        )

    def queries_remote(source):
        return remote(
            own_hbm.at[:, lanes_at(sibling * half_width, half_width)],
            whole.at[plane, x, source],
            local_sem.at[4],
            local_sem.at[5],
            to_sibling,
        )

    def bias_remote(source):
        return remote(bias_out, bias_ref.at[source], local_sem.at[6], local_sem.at[7], to_sibling)

    for which, hbm, ref in kv:
        kv_local(which, hbm, ref, 0).start()
    barrier = pltpu.get_barrier_semaphore()
    greeted = [to_sibling, to_beside] + [index_of(p, x, core) for p in others]
    for device in greeted:
        pl.semaphore_signal(barrier, inc=1, device_id={"ctx": device}, device_id_type=MESH)

    def bias_step(row, _):
        j, t, b = row // (SIDES * key_blocks), row // key_blocks % SIDES, row % key_blocks
        for which, ref in ((core, bias_ref.at[core]), (sibling, bias_out)):
            value = jnp.where(mask_ref[which * each + j, t, b] > 0, 0.0, NEG)
            ref[pl.ds(row, 1), :] = jnp.full((1, LANES), value, jnp.float32)
        return 0

    lax.fori_loop(0, each * SIDES * key_blocks, bias_step, 0)
    pl.semaphore_wait(barrier, len(greeted))
    queries_remote(core).start()
    bias_remote(core).start()
    for which, hbm, ref in kv:
        kv_remote(which, hbm, ref, 0, core).start()

    def gather_plane(j, p, source):
        block = whole.at[source, x, :, :, at_head(j)]
        return remote(
            block,
            block,
            gather_plane_sem.at[0, j, p],
            gather_plane_sem.at[1, j, source],
            index_of(p, x, core),
        )

    def gather_beside(j, t, side):
        block = whole.at[pl.ds(t * span, span), side, :, :, at_head(j)]
        return remote(block, block, gather_sem.at[0, j, t], gather_sem.at[1, j, t], to_beside)

    def gather0(j):
        for p in others:
            gather_plane(j, p, plane).start()

    def gather1(j, t):
        for p in [near] if t is pair else away:
            gather_plane(j, p, p).wait_recv()
        gather_beside(j, t, x).start()

    def gather2(j, t):
        gather_beside(j, t, beside).wait_recv()

    def kv_start(j):
        for which, hbm, ref in kv:
            kv_local(which, hbm, ref, j).start()
            kv_remote(which, hbm, ref, j, core).start()

    def kv_ready(j):
        for which, hbm, ref in kv:
            kv_local(which, hbm, ref, j).wait()
            kv_remote(which, hbm, ref, j, sibling).wait_recv()

    pairs = key_blocks // 2

    def score_item(j, t, score, top_ref):
        tokens = whole.at[pl.ds(t * span, span)]
        query = jnp.concatenate(
            [
                tokens[:, :, :, :, lanes_at(j * wide + g * HEAD_SIZE, HEAD_SIZE)].reshape(
                    query_block, HEAD_SIZE
                )
                for g in range(group)
            ],
            axis=0,
        )
        top = None
        first_row = (j * SIDES + t) * key_blocks
        for which in range(CORES):
            for two in range(pairs):
                at = slice(2 * two * key_block, 2 * (two + 1) * key_block)
                scores = lax.dot_general(
                    query,
                    k_ref[which, at, lanes_at(j * HEAD_SIZE, HEAD_SIZE)],
                    (((1,), (1,)), ((), ())),
                    preferred_element_type=jnp.float32,
                )
                for b in range(2):
                    block = 2 * two + b
                    bias = bias_ref[which, pl.ds(first_row + block, 1), :]
                    part = scores[:, b * key_block : (b + 1) * key_block] + bias
                    to = (which * key_blocks + block) * key_block
                    score[:, to : to + key_block] = part
                    top = part if top is None else jnp.maximum(top, part)
        top = jnp.maximum(jnp.max(top, axis=1, keepdims=True) * factor, LOW)
        top_ref[...] = jnp.broadcast_to(top, top_ref.shape)

    def sum_item(j, t, score, top_ref):
        top = top_ref[...]
        shift = jnp.concatenate([top, top], axis=1)
        both = None
        for which in range(CORES):
            for two in range(pairs):
                at = slice(2 * two * key_block, 2 * (two + 1) * key_block)
                to = (which * key_blocks + 2 * two) * key_block
                probs = jnp.exp2(score[:, to : to + 2 * key_block] * factor - shift).astype(jnp.bfloat16)
                values = jnp.concatenate(
                    [
                        v_ref[which, at, lanes_at(j * HEAD_SIZE, HEAD_SIZE)],
                        jnp.ones((2 * key_block, HEAD_SIZE), jnp.bfloat16),
                    ],
                    axis=1,
                )
                part = jnp.dot(probs, values, preferred_element_type=jnp.float32)
                both = part if both is None else both + part
        split = (group, span, ROW, CORES, rows, HEAD_SIZE)
        numer = both[:, :HEAD_SIZE].reshape(split)
        total = both[:, HEAD_SIZE:].reshape(split)
        tops = top.reshape(split)
        for g in range(group):
            at = slice(g * HEAD_SIZE, (g + 1) * HEAD_SIZE)
            one, two = numer[g, :, 0], numer[g, :, 1]
            mine[j, t, :, :, :, at] = jnp.where(x == 0, one, two)
            beside_out[j, t, :, :, :, at] = jnp.where(x == 0, two, one).astype(jnp.bfloat16)
        lane = lax.broadcasted_iota(jnp.int32, (8, LANES), 1)
        for side in range(ROW):
            tile = jnp.zeros((8, LANES), jnp.float32)
            for q in range(span):
                for which in range(CORES):
                    for half in range(rows // 8):
                        at = slice(half * 8, half * 8 + 8)
                        for g in range(group):
                            to = ((q * CORES + which) * 2 + half) * slots + g
                            tile = jnp.where(lane == to, tops[g, q, side, which, at], tile)
                            to = to + LANES // 2
                            tile = jnp.where(lane == to, total[g, q, side, which, at], tile)
            stat[j, t, side] = tile

    def to_side(j, t):
        return [
            remote(
                beside_out.at[j, t],
                beside_in.at[j, t],
                sum_sem.at[0, j, t],
                sum_sem.at[1, j, t],
                to_beside,
            ),
            remote(
                stat.at[j, t, beside],
                stat_beside_in.at[j, t],
                sum_sem.at[2, j, t],
                sum_sem.at[3, j, t],
                to_beside,
            ),
        ]

    def to_plane(j, t, p, slot):
        device = index_of(p, x, core)
        return [
            remote(
                plane_out.at[j, p],
                plane_in.at[j, slot],
                sum_plane_sem.at[0, j, p],
                sum_plane_sem.at[1, j, slot],
                device,
            ),
            remote(
                stat_merged.at[j, t],
                stat_plane_in.at[j, slot],
                sum_plane_sem.at[2, j, p],
                sum_plane_sem.at[3, j, slot],
                device,
            ),
        ]

    def start(copies):
        for copy in copies:
            copy.start()

    def arrive(copies):
        for copy in copies:
            copy.wait_recv()

    def leave(copies):
        for copy in copies:
            copy.wait_send()

    def sum0(j, t):
        start(to_side(j, t))

    def sum1(j, t):
        arrive(to_side(j, t))
        factors, merged = weigh([stat[j, t, x], stat_beside_in[j, t]])
        stat_merged[j, t] = merged
        for q in range(span):
            values = []
            for which in range(CORES):
                first = (q * CORES + which) * 2 * slots
                parts = []
                for g in range(group):
                    at = slice(g * HEAD_SIZE, (g + 1) * HEAD_SIZE)
                    one, two = [column(tile, first, g, slots) for tile in factors]
                    parts.append(
                        mine[j, t, q, which, :, at] * one
                        + beside_in[j, t, q, which, :, at].astype(jnp.float32) * two
                    )
                values.append(jnp.concatenate(parts, axis=1))
            p = t * span + q

            def keep():
                for which in range(CORES):
                    own[j, which] = values[which]

            def send():
                for which in range(CORES):
                    plane_out[j, p, which] = values[which].astype(jnp.bfloat16)
                start(to_plane(j, t, p, plane))

            if t is pair:
                pl.when(plane == p)(keep)
                pl.when(plane != p)(send)
            else:
                send()

    def swap(j, which, slot):
        head = core * each + j
        device = index_of(head // ROW, head % ROW, which)
        return remote(
            pieces.at[j],
            columns_ref.at[slot // ROW, slot % ROW],
            swap_sem.at[0, j, which],
            swap_sem.at[1, 0, slot],
            device,
        )

    def keep_piece(j):
        return pltpu.make_async_copy(pieces.at[j], columns_ref.at[plane, x], local_sem.at[8])

    slot = plane * ROW + x

    def owner(j, which):
        head = core * each + j
        return index_of(head // ROW, head % ROW, which)

    def sum2(j):
        for p in others:
            arrive(to_plane(j, 0, p, p))
        tiles = [stat_merged[j, pair]] + [stat_plane_in[j, p] for p in others]
        tiles = [jnp.where(odd == 1, swap_quarter(tile), tile) for tile in tiles]
        factors, merged = weigh(tiles)
        merged = swap_halves(merged)
        for which in range(CORES):
            first = which * 2 * slots
            for g in range(group):
                at = slice(g * HEAD_SIZE, (g + 1) * HEAD_SIZE)
                value = own[j, which, :, at] * column(factors[0], first, g, slots)
                for p, one in zip(others, factors[1:]):
                    value = value + plane_in[j, p, which, :, at].astype(jnp.float32) * column(
                        one, first, g, slots
                    )
                value = value / column(merged, first, g, slots)
                pieces[j, which, :, at] = value.astype(jnp.bfloat16)
        for which in range(CORES):

            @pl.when(owner(j, which) == me)
            def _():
                keep_piece(j).start()

            @pl.when(owner(j, which) != me)
            def _():
                swap(j, which, slot).start()

    def swap_quarter(tile):
        return pltpu.roll(tile, LANES - 4 * slots, 1)

    def on(cond, act):
        pl.when(cond)(act)

    queries_in.wait()
    queries_remote(sibling).wait_recv()
    gather0(0)
    gather1(0, pair)
    gather0(1)
    kv_start(1)
    gather1(0, other)
    gather0(2)
    gather1(1, pair)
    bias_remote(sibling).wait_recv()
    kv_ready(0)
    gather2(0, pair)
    score_item(0, pair, score0, top0)

    def head_step(j, _):
        on(j >= 1, lambda: sum0(j - 1, other))
        on(j + 3 < each, lambda: gather0(j + 3))
        on(j + 2 < each, lambda: kv_start(j + 2))
        on(j + 1 < each, lambda: gather1(j + 1, other))
        gather2(j, other)
        on(j >= 2, lambda: sum1(j - 2, other))
        score_item(j, other, score1, top1)
        sum_item(j, pair, score0, top0)
        sum0(j, pair)
        on(j + 2 < each, lambda: gather1(j + 2, pair))

        @pl.when(j + 1 < each)
        def _():
            kv_ready(j + 1)
            gather2(j + 1, pair)

        on(j >= 1, lambda: sum1(j - 1, pair))

        @pl.when(j == 1)
        def _():
            w_local.start()
            w_remote(core).start()

        score_item(jnp.minimum(j + 1, each - 1), pair, score0, top0)
        sum_item(j, other, score1, top1)
        return 0

    lax.fori_loop(0, each, head_step, 0)
    last = each - 1
    for act, *which in (
        (sum0, last, other),
        (sum1, last - 1, other),
        (sum2, 0),
        (sum1, last, pair),
        (sum2, last - 2),
        (sum1, last, other),
        (sum2, last - 1),
        (sum2, last),
    ):
        act(*which)
    w_local.wait()
    w_remote(sibling).wait_recv()

    def take_piece(at, _):
        on(jnp.logical_or(core != pair, at != slot), lambda: swap(0, 0, at).wait_recv())
        return 0

    lax.fori_loop(0, planes * ROW, take_piece, 0)
    on(core == pair, lambda: keep_piece(0).wait())

    tiles = half_width // TILE

    def at_tile(c):
        return lanes_at(c * TILE, TILE)

    def p_side(c):
        return remote(p_out.at[c], p_in.at[c], p_sem.at[0, c], p_sem.at[1, c], to_beside)

    def p_plane(c, p, slot):
        return remote(
            p_plane_out.at[c, p],
            p_plane_in.at[c, slot],
            p_plane_sem.at[0, c, p],
            p_plane_sem.at[1, c, slot],
            index_of(p, x, core),
        )

    def p_end(c, side):
        return remote(
            p_last.at[c],
            out_ref.at[:, lanes_at(side * half_width + c * TILE, TILE)],
            p_sem.at[2, c],
            p_sem.at[3, c],
            to_sibling,
        )

    def project0(c):
        cols = columns_ref[...].reshape(n * rows, wide)
        weight = w_ref[:, :, at_tile(c)].reshape(wide, TILE)
        product = jnp.dot(cols, weight, preferred_element_type=jnp.float32)
        product = product.reshape(planes, ROW, CORES, rows, TILE)
        one, two = product[:, 0], product[:, 1]
        p_out[c] = jnp.where(x == 0, two, one).astype(jnp.bfloat16)
        p_side(c).start()
        p_mine[c] = jnp.where(x == 0, one, two)

    def project1(c):
        p_side(c).wait_recv()
        for p in others:
            value = p_mine[c, p] + p_in[c, p].astype(jnp.float32)
            p_plane_out[c, p] = value.astype(jnp.bfloat16)
            p_plane(c, p, plane).start()
        p_own[c] = p_mine[c, plane] + p_in[c, plane].astype(jnp.float32)

    def project2(c):
        value = p_own[c]
        for p in others:
            p_plane(c, p, p).wait_recv()
        for p in others:
            value = value + p_plane_in[c, p].astype(jnp.float32)
        value = value.astype(jnp.bfloat16)
        p_last[c] = jnp.where(core == 0, value[1], value[0])
        p_end(c, core).start()
        out_ref[:, lanes_at(core * half_width + c * TILE, TILE)] = jnp.where(
            core == 0, value[0], value[1]
        )

    def loop(count, act):
        def step(c, _):
            act(c)
            return 0

        lax.fori_loop(0, count, step, 0)

    loop(tiles, project0)
    loop(tiles, project1)
    loop(tiles, project2)

    def p_drain(c):
        p_end(c, sibling).wait_recv()
        p_end(c, core).wait_send()
        p_side(c).wait_send()
        for p in others:
            p_plane(c, p, plane).wait_send()

    loop(tiles, p_drain)

    def drain(j):
        for p in others:
            gather_plane(j, p, plane).wait_send()
        for t in range(SIDES):
            gather_beside(j, t, x).wait_send()
            leave(to_side(j, t))
        for which, hbm, ref in kv:
            kv_remote(which, hbm, ref, j, core).wait_send()
        for p in others:
            leave(to_plane(j, 0, p, plane))
        for which in range(CORES):
            on(owner(j, which) != me, lambda: swap(j, which, slot).wait_send())

    loop(each, drain)
    queries_remote(core).wait_send()
    bias_remote(core).wait_send()
    w_remote(core).wait_send()


def layer(queries, keys, values, block_mask, weight, n):
    rows, width = queries.shape
    heads, query_blocks, key_blocks = block_mask.shape
    kdev = keys.shape[0]
    planes = n // (CORES * ROW)
    wide = width // heads
    group = wide // HEAD_SIZE
    query_block = n * rows // query_blocks
    span = planes // query_blocks
    each = heads // CORES
    tiles = width // CORES // TILE
    items = (each, query_blocks)
    bf16, f32 = jnp.bfloat16, jnp.float32
    dma = pltpu.SemaphoreType.DMA
    lanes = group * query_block
    shape = (n, planes, heads, group, query_block, key_blocks, kdev // key_blocks)
    tile = (CORES, rows, TILE)
    block = (CORES, rows, wide)
    return pl.pallas_call(
        functools.partial(layer_kernel, shape),
        out_shape=jax.ShapeDtypeStruct((rows, width), bf16),
        in_specs=[
            pl.BlockSpec(memory_space=pl.ANY),
            pl.BlockSpec(memory_space=pl.ANY),
            pl.BlockSpec(memory_space=pl.ANY),
            pl.BlockSpec(memory_space=pltpu.SMEM),
            pl.BlockSpec(memory_space=pl.ANY),
        ],
        out_specs=pl.BlockSpec(memory_space=pltpu.VMEM),
        scratch_shapes=[
            pltpu.VMEM((planes, ROW, CORES, rows, width // CORES), bf16),
            pltpu.VMEM((CORES, kdev, each * HEAD_SIZE), bf16),
            pltpu.VMEM((CORES, kdev, each * HEAD_SIZE), bf16),
            pltpu.VMEM((CORES, weight.shape[0], width // CORES), bf16),
            pltpu.VMEM((CORES, each * query_blocks * key_blocks, LANES), f32),
            pltpu.VMEM((each * query_blocks * key_blocks, LANES), f32),
            pltpu.VMEM((lanes, CORES * kdev), f32),
            pltpu.VMEM((lanes, CORES * kdev), f32),
            pltpu.VMEM((lanes, LANES), f32),
            pltpu.VMEM((lanes, LANES), f32),
            dma((9,)),
            dma((6, each)),
            dma((2, *items)),
            dma((2, each, planes)),
            pltpu.VMEM((*items, span, *block), bf16),
            pltpu.VMEM((*items, span, *block), f32),
            pltpu.VMEM((*items, span, *block), bf16),
            pltpu.VMEM((each, planes, *block), bf16),
            pltpu.VMEM((each, *block), f32),
            pltpu.VMEM((each, planes, *block), bf16),
            pltpu.VMEM((*items, ROW, 8, LANES), f32),
            pltpu.VMEM((*items, 8, LANES), f32),
            pltpu.VMEM((*items, 8, LANES), f32),
            pltpu.VMEM((each, planes, 8, LANES), f32),
            dma((4, *items)),
            dma((4, each, planes)),
            pltpu.VMEM((each, *block), bf16),
            pltpu.VMEM((planes, ROW, *block), bf16),
            dma((2, each, planes * ROW)),
            pltpu.VMEM((tiles, planes, *tile), bf16),
            pltpu.VMEM((tiles, planes, *tile), f32),
            pltpu.VMEM((tiles, planes, *tile), bf16),
            pltpu.VMEM((tiles, planes, *tile), bf16),
            pltpu.VMEM((tiles, *tile), f32),
            pltpu.VMEM((tiles, planes, *tile), bf16),
            pltpu.VMEM((tiles, rows, TILE), bf16),
            dma((4, tiles)),
            dma((2, tiles, planes)),
        ],
        compiler_params=pltpu.CompilerParams(
            collective_id=0, has_side_effects=True, vmem_limit_bytes=60 * 2**20
        ),
        name="layer",
    )(queries, keys, values, block_mask, weight)


def solution(mesh):
    n = mesh.shape["ctx"]

    def shards(queries, keys, values, block_mask, out_weight):
        rows, width = queries.shape
        heads, query_blocks, key_blocks = block_mask.shape
        planes = n // (CORES * ROW)
        group = width // heads // HEAD_SIZE
        fits = (
            n == CORES * ROW * planes
            and n == 2 * heads
            and rows == 16
            and query_blocks == SIDES
            and planes == 2 * SIDES
            and group <= 8
            and key_blocks % 2 == 0
            and width % (CORES * TILE) == 0
        )
        if fits:
            return layer(queries, keys, values, block_mask, out_weight, n)
        return shards_any(queries, keys, values, block_mask, out_weight)

    return jax.shard_map(
        shards,
        mesh=mesh,
        in_specs=(
            P(("groups", "ctx"), None),
            P(("groups", "ctx"), None),
            P(("groups", "ctx"), None),
            P("groups", None, "ctx"),
            P("ctx", None),
        ),
        out_specs=P(("groups", "ctx"), None),
        check_vma=False,
    )
```

```python
import functools
import math

import jax
import jax.numpy as jnp
from jax import lax
from jax.experimental import pallas as pl
from jax.experimental.pallas import tpu as pltpu
from jax.sharding import PartitionSpec as P

HEAD_SIZE = 128
NEG = -1e30
ONES = 16
LOG2E = math.log2(math.e)
MESH = pl.DeviceIdType.MESH
CORES, ROW = 2, 2


def attend_kernel(rows_each, mask_ref, q_ref, k_ref, v_ref, *refs):
    *numer_refs, top_ref, total_ref, live_ref, score_ref, query_ref, value_ref, sum_ref = refs
    head = pl.program_id(0)
    query_blocks, key_blocks = mask_ref.shape[1:]
    key_block = k_ref.shape[0] // key_blocks
    query_block = q_ref.shape[0] // query_blocks
    group = q_ref.shape[1] // HEAD_SIZE
    factor = LOG2E / math.sqrt(HEAD_SIZE)
    value_ref[:HEAD_SIZE] = v_ref[...].T
    value_ref[HEAD_SIZE:] = jnp.ones((ONES, v_ref.shape[0]), jnp.bfloat16)
    for at in range(query_blocks):
        rows = pl.ds(at * query_block, query_block)
        count = jnp.int32(0)
        for block in range(key_blocks):
            live_ref[count] = block
            count = count + (mask_ref[head, at, block] > 0).astype(jnp.int32)
        live_ref[count] = 0
        for g in range(group):
            tokens = q_ref[rows, g * HEAD_SIZE : (g + 1) * HEAD_SIZE]
            query_ref[:, g * query_block : (g + 1) * query_block] = tokens.T
        lanes = query_ref.shape[1]
        pairs = (count + 1) // 2

        def start_of(which):
            return pl.multiple_of(live_ref[which] * key_block, key_block)

        eights, quads = (count + 1) // 8, (count + 1) // 4

        def taken(ref_slice, first, blocks, axis):
            return jnp.concatenate([ref_slice(start_of(first + b)) for b in range(blocks)], axis=axis)

        def score_step(blocks, step, top):
            pair = step * (blocks // 2)
            keys = taken(lambda at: k_ref[pl.ds(at, key_block), :], 2 * pair, blocks, 0)
            scores = jnp.dot(keys, query_ref[...], preferred_element_type=jnp.float32)
            score_ref[pl.ds(pair, blocks // 2)] = scores.reshape(blocks // 2, 2 * key_block, lanes)
            tops = jnp.max(scores.reshape(blocks, key_block // 8, 8, lanes), axis=1)
            for b in range(blocks):
                one = tops[b]
                if b == blocks - 1:
                    one = jnp.where(2 * pair + b < count, one, NEG)
                top = jnp.maximum(top, one)
            return top

        top = jnp.full((8, lanes), NEG, jnp.float32)
        top = lax.fori_loop(0, eights, functools.partial(score_step, 8), top)
        top = lax.fori_loop(2 * eights, quads, functools.partial(score_step, 4), top)
        top = lax.fori_loop(2 * quads, pairs, functools.partial(score_step, 2), top)
        top = jnp.max(top, axis=0, keepdims=True) * factor
        sum_ref[...] = jnp.zeros_like(sum_ref)

        def sum_step(blocks, step, _):
            pair = step * (blocks // 2)
            probs = []
            for b in range(blocks):
                shift = top
                if b == blocks - 1:
                    shift = jnp.where(2 * pair + b < count, top, -NEG)
                half = slice(b % 2 * key_block, (b % 2 + 1) * key_block)
                scores = score_ref[pair + b // 2, half]
                probs.append(jnp.exp2(scores * factor - shift).astype(jnp.bfloat16))
            values = taken(lambda at: value_ref[:, pl.ds(at, key_block)], 2 * pair, blocks, 1)
            sum_ref[...] += jnp.dot(
                values, jnp.concatenate(probs, axis=0), preferred_element_type=jnp.float32
            )
            return 0

        lax.fori_loop(0, eights, functools.partial(sum_step, 8), 0)
        lax.fori_loop(2 * eights, quads, functools.partial(sum_step, 4), 0)
        lax.fori_loop(2 * quads, pairs, functools.partial(sum_step, 2), 0)
        numer = sum_ref[:HEAD_SIZE]
        top_ref[0, at : at + 1, :] = top
        total_ref[0, at : at + 1, :] = sum_ref[HEAD_SIZE : HEAD_SIZE + 1]
        for g in range(group):
            columns = slice(g * query_block, (g + 1) * query_block)
            out_columns = slice(g * HEAD_SIZE, (g + 1) * HEAD_SIZE)
            tokens = numer[:, columns].T
            if not rows_each:
                numer_refs[0][rows, out_columns] = tokens
                continue
            tokens = tokens.reshape(-1, CORES, rows_each, HEAD_SIZE)
            first = lax.rem(lax.axis_index("ctx"), CORES) == 0
            half = pl.ds(at * query_block // CORES, query_block // CORES)
            kept = jnp.where(first, tokens[:, 0], tokens[:, 1]).reshape(-1, HEAD_SIZE)
            sent = jnp.where(first, tokens[:, 1], tokens[:, 0]).reshape(-1, HEAD_SIZE)
            numer_refs[0][half, out_columns] = kept
            numer_refs[1][half, out_columns] = sent.astype(jnp.bfloat16)


def attend(whole, keys, values, block_mask, rows_each):
    qtok, width = whole.shape
    kdev = keys.shape[0]
    heads_kv, query_blocks, key_blocks = block_mask.shape
    columns = width // heads_kv
    lanes = columns // HEAD_SIZE * (qtok // query_blocks)
    stat = jax.ShapeDtypeStruct((heads_kv, query_blocks, lanes), jnp.float32)
    stat_spec = pl.BlockSpec((1, query_blocks, lanes), lambda h: (h, 0, 0))
    numers = [jax.ShapeDtypeStruct((qtok, width), jnp.float32)]
    if rows_each:
        numers = [jax.ShapeDtypeStruct((qtok // CORES, width), t) for t in (jnp.float32, jnp.bfloat16)]
    return pl.pallas_call(
        functools.partial(attend_kernel, rows_each),
        grid=(heads_kv,),
        out_shape=(*numers, stat, stat),
        in_specs=[
            pl.BlockSpec(memory_space=pltpu.SMEM),
            pl.BlockSpec((qtok, columns), lambda h: (0, h)),
            pl.BlockSpec((kdev, HEAD_SIZE), lambda h: (0, h)),
            pl.BlockSpec((kdev, HEAD_SIZE), lambda h: (0, h)),
        ],
        out_specs=(
            *(pl.BlockSpec((numer.shape[0], columns), lambda h: (0, h)) for numer in numers),
            stat_spec,
            stat_spec,
        ),
        scratch_shapes=[
            pltpu.SMEM((key_blocks + 2,), jnp.int32),
            pltpu.VMEM(((key_blocks + 1) // 2, 2 * kdev // key_blocks, lanes), jnp.float32),
            pltpu.VMEM((HEAD_SIZE, lanes), jnp.bfloat16),
            pltpu.VMEM((HEAD_SIZE + ONES, kdev), jnp.bfloat16),
            pltpu.VMEM((HEAD_SIZE + ONES, lanes), jnp.float32),
        ],
        compiler_params=pltpu.CompilerParams(vmem_limit_bytes=60 * 2**20),
        name="attend",
    )(block_mask, whole, keys, values)


def by_token(stat, qtok):
    heads_kv, query_blocks, _ = stat.shape
    stat = stat.reshape(heads_kv, query_blocks, -1, qtok // query_blocks)
    return stat.transpose(1, 3, 0, 2).reshape(qtok, -1)


def shards_any(queries, keys, values, block_mask, out_weight):
    whole = lax.all_gather(queries, "ctx", axis=0, tiled=True)
    qtok, width = whole.shape
    numer, top, total = attend(whole, keys, values, block_mask, 0)
    rescale = by_token(jnp.exp2(top - lax.pmax(top, "ctx")), qtok)
    denom = by_token(total, qtok) * rescale
    numer = (numer.reshape(qtok, -1, HEAD_SIZE) * rescale[:, :, None]).reshape(qtok, width)
    num_rows = lax.psum_scatter(numer, "ctx", scatter_dimension=0, tiled=True)
    den_rows = lax.psum_scatter(denom, "ctx", scatter_dimension=0, tiled=True)
    own_rows = num_rows.shape[0]
    attn_rows = (num_rows.reshape(own_rows, -1, HEAD_SIZE) / den_rows[:, :, None]).reshape(
        own_rows, width
    )
    attn_cols = lax.all_to_all(
        attn_rows.astype(jnp.bfloat16), "ctx", split_axis=1, concat_axis=0, tiled=True
    )
    summed = lax.psum_scatter(
        jnp.dot(attn_cols, out_weight, preferred_element_type=jnp.float32),
        "ctx",
        scatter_dimension=0,
        tiled=True,
    )
    return summed.astype(jnp.bfloat16)


def place(n):
    me = lax.axis_index("ctx")
    core = lax.rem(me, CORES)
    x = lax.rem(me // CORES, ROW)
    plane = me // (CORES * ROW)
    return me, plane, x, core


def index_of(plane, x, core):
    return (plane * ROW + x) * CORES + core


def remote(src, dst, send, recv, device):
    return pltpu.make_async_remote_copy(
        src_ref=src,
        dst_ref=dst,
        send_sem=send,
        recv_sem=recv,
        device_id={"ctx": device},
        device_id_type=MESH,
    )


LOW = -1e28
LANES = 128
SIDES = 2
TILE = 512


def swap_halves(stat):
    return pltpu.roll(stat, LANES // 2, 1)


def weigh(stats):
    lane = lax.broadcasted_iota(jnp.int32, stats[0].shape, 1)
    top = functools.reduce(jnp.maximum, stats)
    factors = [jnp.exp2(stat - top) for stat in stats]
    total = sum(stat * swap_halves(factor) for stat, factor in zip(stats, factors))
    return factors, jnp.where(lane < LANES // 2, top, total)


def column(tile, first, g, slots):
    lanes = [first + half * slots + g for half in range(2)]
    return jnp.concatenate([tile[:, lane : lane + 1] for lane in lanes], axis=0)


def layer_kernel(
    shape,
    own_hbm,
    k_hbm,
    v_hbm,
    mask_ref,
    w_hbm,
    out_ref,
    whole,
    k_ref,
    v_ref,
    w_ref,
    bias_ref,
    bias_out,
    score0,
    score1,
    top0,
    top1,
    local_sem,
    kv_sem,
    gather_sem,
    gather_plane_sem,
    beside_out,
    mine,
    beside_in,
    plane_out,
    own,
    plane_in,
    stat,
    stat_beside_in,
    stat_merged,
    stat_plane_in,
    sum_sem,
    sum_plane_sem,
    pieces,
    columns_ref,
    swap_sem,
    p_out,
    p_mine,
    p_in,
    p_plane_out,
    p_own,
    p_plane_in,
    p_last,
    p_sem,
    p_plane_sem,
):
    n, planes, heads, group, query_block, key_blocks, key_block = shape
    me, plane, x, core = place(n)
    beside, sibling = 1 - x, 1 - core
    rows = own_hbm.shape[0]
    span = planes // SIDES
    wide = group * HEAD_SIZE
    each = heads // CORES
    factor = LOG2E / math.sqrt(HEAD_SIZE)
    slots = 8
    pair, odd = plane // span, lax.rem(plane, span)
    near = pair * span + 1 - odd
    other = 1 - pair
    away = [other * span + odd, other * span + 1 - odd]
    others = [near] + away
    to_beside = index_of(plane, beside, core)
    to_sibling = index_of(plane, x, sibling)

    def lanes_at(start, width, unit=LANES):
        return pl.ds(pl.multiple_of(start, unit), width)

    def at_head(j):
        return lanes_at(j * wide, wide)

    half_width = each * wide
    queries_in = pltpu.make_async_copy(
        own_hbm.at[:, lanes_at(core * half_width, half_width)], whole.at[plane, x, core], local_sem.at[0]
    )
    queries_in.start()

    def kv_local(which, hbm, ref, j):
        return pltpu.make_async_copy(
            hbm.at[:, lanes_at((core * each + j) * HEAD_SIZE, HEAD_SIZE)],
            ref.at[core, :, lanes_at(j * HEAD_SIZE, HEAD_SIZE)],
            kv_sem.at[which, j],
        )

    def kv_remote(which, hbm, ref, j, source):
        return remote(
            hbm.at[:, lanes_at((sibling * each + j) * HEAD_SIZE, HEAD_SIZE)],
            ref.at[source, :, lanes_at(j * HEAD_SIZE, HEAD_SIZE)],
            kv_sem.at[2 + which, j],
            kv_sem.at[4 + which, j],
            to_sibling,
        )

    kv = [(0, k_hbm, k_ref), (1, v_hbm, v_ref)]
    w_local = pltpu.make_async_copy(
        w_hbm.at[:, lanes_at(core * half_width, half_width)], w_ref.at[core], local_sem.at[1]
    )

    def w_remote(source):
        return remote(
            w_hbm.at[:, lanes_at(sibling * half_width, half_width)],
            w_ref.at[source],
            local_sem.at[2],
            local_sem.at[3],
            to_sibling,
        )

    def queries_remote(source):
        return remote(
            own_hbm.at[:, lanes_at(sibling * half_width, half_width)],
            whole.at[plane, x, source],
            local_sem.at[4],
            local_sem.at[5],
            to_sibling,
        )

    def bias_remote(source):
        return remote(bias_out, bias_ref.at[source], local_sem.at[6], local_sem.at[7], to_sibling)

    for which, hbm, ref in kv:
        kv_local(which, hbm, ref, 0).start()
    barrier = pltpu.get_barrier_semaphore()
    greeted = [to_sibling, to_beside] + [index_of(p, x, core) for p in others]
    for device in greeted:
        pl.semaphore_signal(barrier, inc=1, device_id={"ctx": device}, device_id_type=MESH)

    def bias_step(row, _):
        j, t, b = row // (SIDES * key_blocks), row // key_blocks % SIDES, row % key_blocks
        for which, ref in ((core, bias_ref.at[core]), (sibling, bias_out)):
            value = jnp.where(mask_ref[which * each + j, t, b] > 0, 0.0, NEG)
            ref[pl.ds(row, 1), :] = jnp.full((1, LANES), value, jnp.float32)
        return 0

    lax.fori_loop(0, each * SIDES * key_blocks, bias_step, 0)
    pl.semaphore_wait(barrier, len(greeted))
    queries_remote(core).start()
    bias_remote(core).start()
    for which, hbm, ref in kv:
        kv_remote(which, hbm, ref, 0, core).start()

    def gather_plane(j, p, source):
        block = whole.at[source, x, :, :, at_head(j)]
        return remote(
            block,
            block,
            gather_plane_sem.at[0, j, p],
            gather_plane_sem.at[1, j, source],
            index_of(p, x, core),
        )

    def gather_beside(j, t, side):
        block = whole.at[pl.ds(t * span, span), side, :, :, at_head(j)]
        return remote(block, block, gather_sem.at[0, j, t], gather_sem.at[1, j, t], to_beside)

    def gather0(j):
        for p in others:
            gather_plane(j, p, plane).start()

    def gather1(j, t):
        for p in [near] if t is pair else away:
            gather_plane(j, p, p).wait_recv()
        gather_beside(j, t, x).start()

    def gather2(j, t):
        gather_beside(j, t, beside).wait_recv()

    def kv_start(j):
        for which, hbm, ref in kv:
            kv_local(which, hbm, ref, j).start()
            kv_remote(which, hbm, ref, j, core).start()

    def kv_ready(j):
        for which, hbm, ref in kv:
            kv_local(which, hbm, ref, j).wait()
            kv_remote(which, hbm, ref, j, sibling).wait_recv()

    pairs = key_blocks // 2

    def score_item(j, t, score, top_ref):
        tokens = whole.at[pl.ds(t * span, span)]
        query = jnp.concatenate(
            [
                tokens[:, :, :, :, lanes_at(j * wide + g * HEAD_SIZE, HEAD_SIZE)].reshape(
                    query_block, HEAD_SIZE
                )
                for g in range(group)
            ],
            axis=0,
        )
        top = None
        first_row = (j * SIDES + t) * key_blocks
        for which in range(CORES):
            for two in range(pairs):
                at = slice(2 * two * key_block, 2 * (two + 1) * key_block)
                scores = lax.dot_general(
                    query,
                    k_ref[which, at, lanes_at(j * HEAD_SIZE, HEAD_SIZE)],
                    (((1,), (1,)), ((), ())),
                    preferred_element_type=jnp.float32,
                )
                for b in range(2):
                    block = 2 * two + b
                    bias = bias_ref[which, pl.ds(first_row + block, 1), :]
                    part = scores[:, b * key_block : (b + 1) * key_block] + bias
                    to = (which * key_blocks + block) * key_block
                    score[:, to : to + key_block] = part
                    top = part if top is None else jnp.maximum(top, part)
        top = jnp.maximum(jnp.max(top, axis=1, keepdims=True) * factor, LOW)
        top_ref[...] = jnp.broadcast_to(top, top_ref.shape)

    def sum_item(j, t, score, top_ref):
        top = top_ref[...]
        shift = jnp.concatenate([top, top], axis=1)
        both = None
        for which in range(CORES):
            for two in range(pairs):
                at = slice(2 * two * key_block, 2 * (two + 1) * key_block)
                to = (which * key_blocks + 2 * two) * key_block
                probs = jnp.exp2(score[:, to : to + 2 * key_block] * factor - shift).astype(jnp.bfloat16)
                values = jnp.concatenate(
                    [
                        v_ref[which, at, lanes_at(j * HEAD_SIZE, HEAD_SIZE)],
                        jnp.ones((2 * key_block, HEAD_SIZE), jnp.bfloat16),
                    ],
                    axis=1,
                )
                part = jnp.dot(probs, values, preferred_element_type=jnp.float32)
                both = part if both is None else both + part
        split = (group, span, ROW, CORES, rows, HEAD_SIZE)
        numer = both[:, :HEAD_SIZE].reshape(split)
        total = both[:, HEAD_SIZE:].reshape(split)
        tops = top.reshape(split)
        for g in range(group):
            at = slice(g * HEAD_SIZE, (g + 1) * HEAD_SIZE)
            one, two = numer[g, :, 0], numer[g, :, 1]
            mine[j, t, :, :, :, at] = jnp.where(x == 0, one, two)
            beside_out[j, t, :, :, :, at] = jnp.where(x == 0, two, one).astype(jnp.bfloat16)
        lane = lax.broadcasted_iota(jnp.int32, (8, LANES), 1)
        for side in range(ROW):
            tile = jnp.zeros((8, LANES), jnp.float32)
            for q in range(span):
                for which in range(CORES):
                    for half in range(rows // 8):
                        at = slice(half * 8, half * 8 + 8)
                        for g in range(group):
                            to = ((q * CORES + which) * 2 + half) * slots + g
                            tile = jnp.where(lane == to, tops[g, q, side, which, at], tile)
                            to = to + LANES // 2
                            tile = jnp.where(lane == to, total[g, q, side, which, at], tile)
            stat[j, t, side] = tile

    def to_side(j, t):
        return [
            remote(
                beside_out.at[j, t],
                beside_in.at[j, t],
                sum_sem.at[0, j, t],
                sum_sem.at[1, j, t],
                to_beside,
            ),
            remote(
                stat.at[j, t, beside],
                stat_beside_in.at[j, t],
                sum_sem.at[2, j, t],
                sum_sem.at[3, j, t],
                to_beside,
            ),
        ]

    def to_plane(j, t, p, slot):
        device = index_of(p, x, core)
        return [
            remote(
                plane_out.at[j, p],
                plane_in.at[j, slot],
                sum_plane_sem.at[0, j, p],
                sum_plane_sem.at[1, j, slot],
                device,
            ),
            remote(
                stat_merged.at[j, t],
                stat_plane_in.at[j, slot],
                sum_plane_sem.at[2, j, p],
                sum_plane_sem.at[3, j, slot],
                device,
            ),
        ]

    def start(copies):
        for copy in copies:
            copy.start()

    def arrive(copies):
        for copy in copies:
            copy.wait_recv()

    def leave(copies):
        for copy in copies:
            copy.wait_send()

    def sum0(j, t):
        start(to_side(j, t))

    def sum1(j, t):
        arrive(to_side(j, t))
        factors, merged = weigh([stat[j, t, x], stat_beside_in[j, t]])
        stat_merged[j, t] = merged
        for q in range(span):
            values = []
            for which in range(CORES):
                first = (q * CORES + which) * 2 * slots
                parts = []
                for g in range(group):
                    at = slice(g * HEAD_SIZE, (g + 1) * HEAD_SIZE)
                    one, two = [column(tile, first, g, slots) for tile in factors]
                    parts.append(
                        mine[j, t, q, which, :, at] * one
                        + beside_in[j, t, q, which, :, at].astype(jnp.float32) * two
                    )
                values.append(jnp.concatenate(parts, axis=1))
            p = t * span + q

            def keep():
                for which in range(CORES):
                    own[j, which] = values[which]

            def send():
                for which in range(CORES):
                    plane_out[j, p, which] = values[which].astype(jnp.bfloat16)
                start(to_plane(j, t, p, plane))

            if t is pair:
                pl.when(plane == p)(keep)
                pl.when(plane != p)(send)
            else:
                send()

    def swap(j, which, slot):
        head = core * each + j
        device = index_of(head // ROW, head % ROW, 1 - which)
        return remote(
            pieces.at[j, which],
            columns_ref.at[slot // ROW, slot % ROW, which],
            swap_sem.at[0, j, which],
            swap_sem.at[1, 0, slot],
            device,
        )

    def keep_piece(j):
        return pltpu.make_async_copy(
            pieces.at[j, sibling], columns_ref.at[plane, x, sibling], local_sem.at[8]
        )

    def columns_on(which):
        block = columns_ref.at[:, :, which]
        return remote(block, block, local_sem.at[9], local_sem.at[10], to_sibling)

    slot = plane * ROW + x

    def owner(j, which):
        head = core * each + j
        return index_of(head // ROW, head % ROW, 1 - which)

    def sum2(j):
        for p in others:
            arrive(to_plane(j, 0, p, p))
        tiles = [stat_merged[j, pair]] + [stat_plane_in[j, p] for p in others]
        tiles = [jnp.where(odd == 1, swap_quarter(tile), tile) for tile in tiles]
        factors, merged = weigh(tiles)
        merged = swap_halves(merged)
        for which in range(CORES):
            first = which * 2 * slots
            for g in range(group):
                at = slice(g * HEAD_SIZE, (g + 1) * HEAD_SIZE)
                value = own[j, which, :, at] * column(factors[0], first, g, slots)
                for p, one in zip(others, factors[1:]):
                    value = value + plane_in[j, p, which, :, at].astype(jnp.float32) * column(
                        one, first, g, slots
                    )
                value = value / column(merged, first, g, slots)
                pieces[j, which, :, at] = value.astype(jnp.bfloat16)
        for which in range(CORES):

            @pl.when(owner(j, which) == me)
            def _():
                keep_piece(j).start()

            @pl.when(owner(j, which) != me)
            def _():
                swap(j, which, slot).start()

    def swap_quarter(tile):
        return pltpu.roll(tile, LANES - 4 * slots, 1)

    def on(cond, act):
        pl.when(cond)(act)

    queries_in.wait()
    queries_remote(sibling).wait_recv()
    gather0(0)
    gather1(0, pair)
    gather0(1)
    kv_start(1)
    gather1(0, other)
    gather0(2)
    gather1(1, pair)
    bias_remote(sibling).wait_recv()
    kv_ready(0)
    gather2(0, pair)
    score_item(0, pair, score0, top0)

    def head_step(j, _):
        on(j >= 1, lambda: sum0(j - 1, other))
        on(j + 3 < each, lambda: gather0(j + 3))
        on(j + 2 < each, lambda: kv_start(j + 2))
        on(j + 1 < each, lambda: gather1(j + 1, other))
        gather2(j, other)
        on(j >= 2, lambda: sum1(j - 2, other))
        score_item(j, other, score1, top1)
        sum_item(j, pair, score0, top0)
        sum0(j, pair)
        on(j + 2 < each, lambda: gather1(j + 2, pair))

        @pl.when(j + 1 < each)
        def _():
            kv_ready(j + 1)
            gather2(j + 1, pair)

        on(j >= 1, lambda: sum1(j - 1, pair))

        @pl.when(j == 1)
        def _():
            w_local.start()
            w_remote(core).start()

        score_item(jnp.minimum(j + 1, each - 1), pair, score0, top0)
        sum_item(j, other, score1, top1)
        return 0

    lax.fori_loop(0, each, head_step, 0)
    last = each - 1
    for act, *which in (
        (sum0, last, other),
        (sum1, last - 1, other),
        (sum2, 0),
        (sum1, last, pair),
        (sum2, last - 2),
        (sum1, last, other),
        (sum2, last - 1),
        (sum2, last),
    ):
        act(*which)
    w_local.wait()
    w_remote(sibling).wait_recv()

    def take_piece(at, _):
        on(jnp.logical_or(core != pair, at != slot), lambda: swap(0, sibling, at).wait_recv())
        return 0

    lax.fori_loop(0, planes * ROW, take_piece, 0)
    on(core == pair, lambda: keep_piece(0).wait())
    columns_on(sibling).start()

    tiles = half_width // TILE
    units = 2 * tiles

    def p_side(u):
        return remote(p_out.at[u], p_in.at[u], p_sem.at[0, u], p_sem.at[1, u], to_beside)

    def p_plane(u, p, slot):
        return remote(
            p_plane_out.at[u, p],
            p_plane_in.at[u, slot],
            p_plane_sem.at[0, u, p],
            p_plane_sem.at[1, u, slot],
            index_of(p, x, core),
        )

    def out_at(side, c):
        return out_ref.at[:, lanes_at(side * half_width + c * TILE, TILE)]

    def p_end(c, side):
        return remote(p_last.at[c], out_at(side, c), p_sem.at[2, c], p_sem.at[3, c], to_sibling)

    def project0(c, which, u):
        cols = columns_ref[:, :, which].reshape(planes * ROW * rows, wide)
        weight = w_ref[:, :, lanes_at(c * TILE, TILE)].reshape(wide, TILE)
        product = jnp.dot(cols, weight, preferred_element_type=jnp.float32)
        product = product.reshape(planes, ROW, rows, TILE)
        one, two = product[:, 0], product[:, 1]
        p_out[u] = jnp.where(x == 0, two, one).astype(jnp.bfloat16)
        p_side(u).start()
        p_mine[u] = jnp.where(x == 0, one, two)

    def project1(u):
        p_side(u).wait_recv()
        for p in others:
            value = p_mine[u, p] + p_in[u, p].astype(jnp.float32)
            p_plane_out[u, p] = value.astype(jnp.bfloat16)
            p_plane(u, p, plane).start()
        p_own[u] = p_mine[u, plane] + p_in[u, plane].astype(jnp.float32)

    def project2(u):
        value = p_own[u]
        for p in others:
            p_plane(u, p, p).wait_recv()
        for p in others:
            value = value + p_plane_in[u, p].astype(jnp.float32)
        return value.astype(jnp.bfloat16)

    def loop(count, act):
        def step(c, _):
            act(c)
            return 0

        lax.fori_loop(0, count, step, 0)

    def finish_sibling(c):
        p_last[c] = project2(c)
        p_end(c, core).start()

    def finish_own(c):
        out_ref[:, lanes_at(core * half_width + c * TILE, TILE)] = project2(tiles + c)

    loop(tiles, lambda c: project0(c, sibling, c))
    columns_on(core).wait_recv()
    loop(tiles, lambda c: project0(c, core, tiles + c))
    loop(units, project1)
    loop(tiles, finish_sibling)
    loop(tiles, finish_own)

    def p_drain(c):
        p_end(c, sibling).wait_recv()
        p_end(c, core).wait_send()

    def u_drain(u):
        p_side(u).wait_send()
        for p in others:
            p_plane(u, p, plane).wait_send()

    loop(tiles, p_drain)
    loop(units, u_drain)
    columns_on(sibling).wait_send()

    def drain(j):
        for p in others:
            gather_plane(j, p, plane).wait_send()
        for t in range(SIDES):
            gather_beside(j, t, x).wait_send()
            leave(to_side(j, t))
        for which, hbm, ref in kv:
            kv_remote(which, hbm, ref, j, core).wait_send()
        for p in others:
            leave(to_plane(j, 0, p, plane))
        for which in range(CORES):
            on(owner(j, which) != me, lambda: swap(j, which, slot).wait_send())

    loop(each, drain)
    queries_remote(core).wait_send()
    bias_remote(core).wait_send()
    w_remote(core).wait_send()


def layer(queries, keys, values, block_mask, weight, n):
    rows, width = queries.shape
    heads, query_blocks, key_blocks = block_mask.shape
    kdev = keys.shape[0]
    planes = n // (CORES * ROW)
    wide = width // heads
    group = wide // HEAD_SIZE
    query_block = n * rows // query_blocks
    span = planes // query_blocks
    each = heads // CORES
    tiles = width // CORES // TILE
    items = (each, query_blocks)
    bf16, f32 = jnp.bfloat16, jnp.float32
    dma = pltpu.SemaphoreType.DMA
    lanes = group * query_block
    shape = (n, planes, heads, group, query_block, key_blocks, kdev // key_blocks)
    tile = (rows, TILE)
    units = CORES * tiles
    block = (CORES, rows, wide)
    return pl.pallas_call(
        functools.partial(layer_kernel, shape),
        out_shape=jax.ShapeDtypeStruct((rows, width), bf16),
        in_specs=[
            pl.BlockSpec(memory_space=pl.ANY),
            pl.BlockSpec(memory_space=pl.ANY),
            pl.BlockSpec(memory_space=pl.ANY),
            pl.BlockSpec(memory_space=pltpu.SMEM),
            pl.BlockSpec(memory_space=pl.ANY),
        ],
        out_specs=pl.BlockSpec(memory_space=pltpu.VMEM),
        scratch_shapes=[
            pltpu.VMEM((planes, ROW, CORES, rows, width // CORES), bf16),
            pltpu.VMEM((CORES, kdev, each * HEAD_SIZE), bf16),
            pltpu.VMEM((CORES, kdev, each * HEAD_SIZE), bf16),
            pltpu.VMEM((CORES, weight.shape[0], width // CORES), bf16),
            pltpu.VMEM((CORES, each * query_blocks * key_blocks, LANES), f32),
            pltpu.VMEM((each * query_blocks * key_blocks, LANES), f32),
            pltpu.VMEM((lanes, CORES * kdev), f32),
            pltpu.VMEM((lanes, CORES * kdev), f32),
            pltpu.VMEM((lanes, LANES), f32),
            pltpu.VMEM((lanes, LANES), f32),
            dma((11,)),
            dma((6, each)),
            dma((2, *items)),
            dma((2, each, planes)),
            pltpu.VMEM((*items, span, *block), bf16),
            pltpu.VMEM((*items, span, *block), f32),
            pltpu.VMEM((*items, span, *block), bf16),
            pltpu.VMEM((each, planes, *block), bf16),
            pltpu.VMEM((each, *block), f32),
            pltpu.VMEM((each, planes, *block), bf16),
            pltpu.VMEM((*items, ROW, 8, LANES), f32),
            pltpu.VMEM((*items, 8, LANES), f32),
            pltpu.VMEM((*items, 8, LANES), f32),
            pltpu.VMEM((each, planes, 8, LANES), f32),
            dma((4, *items)),
            dma((4, each, planes)),
            pltpu.VMEM((each, *block), bf16),
            pltpu.VMEM((planes, ROW, *block), bf16),
            dma((2, each, planes * ROW)),
            pltpu.VMEM((units, planes, *tile), bf16),
            pltpu.VMEM((units, planes, *tile), f32),
            pltpu.VMEM((units, planes, *tile), bf16),
            pltpu.VMEM((units, planes, *tile), bf16),
            pltpu.VMEM((units, *tile), f32),
            pltpu.VMEM((units, planes, *tile), bf16),
            pltpu.VMEM((tiles, *tile), bf16),
            dma((4, units)),
            dma((2, units, planes)),
        ],
        compiler_params=pltpu.CompilerParams(
            collective_id=0, has_side_effects=True, vmem_limit_bytes=60 * 2**20
        ),
        name="layer",
    )(queries, keys, values, block_mask, weight)


def solution(mesh):
    n = mesh.shape["ctx"]

    def shards(queries, keys, values, block_mask, out_weight):
        rows, width = queries.shape
        heads, query_blocks, key_blocks = block_mask.shape
        planes = n // (CORES * ROW)
        group = width // heads // HEAD_SIZE
        fits = (
            n == CORES * ROW * planes
            and n == 2 * heads
            and rows == 16
            and query_blocks == SIDES
            and planes == 2 * SIDES
            and group <= 8
            and key_blocks % 2 == 0
            and width % (CORES * TILE) == 0
        )
        if fits:
            return layer(queries, keys, values, block_mask, out_weight, n)
        return shards_any(queries, keys, values, block_mask, out_weight)

    return jax.shard_map(
        shards,
        mesh=mesh,
        in_specs=(
            P(("groups", "ctx"), None),
            P(("groups", "ctx"), None),
            P(("groups", "ctx"), None),
            P("groups", None, "ctx"),
            P("ctx", None),
        ),
        out_specs=P(("groups", "ctx"), None),
        check_vma=False,
    )
```

```python
import functools
import math

import jax
import jax.numpy as jnp
from jax import lax
from jax.experimental import pallas as pl
from jax.experimental.pallas import tpu as pltpu
from jax.sharding import PartitionSpec as P

HEAD_SIZE = 128
NEG = -1e30
ONES = 16
LOG2E = math.log2(math.e)
MESH = pl.DeviceIdType.MESH
CORES, ROW = 2, 2


def attend_kernel(rows_each, mask_ref, q_ref, k_ref, v_ref, *refs):
    *numer_refs, top_ref, total_ref, live_ref, score_ref, query_ref, value_ref, sum_ref = refs
    head = pl.program_id(0)
    query_blocks, key_blocks = mask_ref.shape[1:]
    key_block = k_ref.shape[0] // key_blocks
    query_block = q_ref.shape[0] // query_blocks
    group = q_ref.shape[1] // HEAD_SIZE
    factor = LOG2E / math.sqrt(HEAD_SIZE)
    value_ref[:HEAD_SIZE] = v_ref[...].T
    value_ref[HEAD_SIZE:] = jnp.ones((ONES, v_ref.shape[0]), jnp.bfloat16)
    for at in range(query_blocks):
        rows = pl.ds(at * query_block, query_block)
        count = jnp.int32(0)
        for block in range(key_blocks):
            live_ref[count] = block
            count = count + (mask_ref[head, at, block] > 0).astype(jnp.int32)
        live_ref[count] = 0
        for g in range(group):
            tokens = q_ref[rows, g * HEAD_SIZE : (g + 1) * HEAD_SIZE]
            query_ref[:, g * query_block : (g + 1) * query_block] = tokens.T
        lanes = query_ref.shape[1]
        pairs = (count + 1) // 2

        def start_of(which):
            return pl.multiple_of(live_ref[which] * key_block, key_block)

        eights, quads = (count + 1) // 8, (count + 1) // 4

        def taken(ref_slice, first, blocks, axis):
            return jnp.concatenate([ref_slice(start_of(first + b)) for b in range(blocks)], axis=axis)

        def score_step(blocks, step, top):
            pair = step * (blocks // 2)
            keys = taken(lambda at: k_ref[pl.ds(at, key_block), :], 2 * pair, blocks, 0)
            scores = jnp.dot(keys, query_ref[...], preferred_element_type=jnp.float32)
            score_ref[pl.ds(pair, blocks // 2)] = scores.reshape(blocks // 2, 2 * key_block, lanes)
            tops = jnp.max(scores.reshape(blocks, key_block // 8, 8, lanes), axis=1)
            for b in range(blocks):
                one = tops[b]
                if b == blocks - 1:
                    one = jnp.where(2 * pair + b < count, one, NEG)
                top = jnp.maximum(top, one)
            return top

        top = jnp.full((8, lanes), NEG, jnp.float32)
        top = lax.fori_loop(0, eights, functools.partial(score_step, 8), top)
        top = lax.fori_loop(2 * eights, quads, functools.partial(score_step, 4), top)
        top = lax.fori_loop(2 * quads, pairs, functools.partial(score_step, 2), top)
        top = jnp.max(top, axis=0, keepdims=True) * factor
        sum_ref[...] = jnp.zeros_like(sum_ref)

        def sum_step(blocks, step, _):
            pair = step * (blocks // 2)
            probs = []
            for b in range(blocks):
                shift = top
                if b == blocks - 1:
                    shift = jnp.where(2 * pair + b < count, top, -NEG)
                half = slice(b % 2 * key_block, (b % 2 + 1) * key_block)
                scores = score_ref[pair + b // 2, half]
                probs.append(jnp.exp2(scores * factor - shift).astype(jnp.bfloat16))
            values = taken(lambda at: value_ref[:, pl.ds(at, key_block)], 2 * pair, blocks, 1)
            sum_ref[...] += jnp.dot(
                values, jnp.concatenate(probs, axis=0), preferred_element_type=jnp.float32
            )
            return 0

        lax.fori_loop(0, eights, functools.partial(sum_step, 8), 0)
        lax.fori_loop(2 * eights, quads, functools.partial(sum_step, 4), 0)
        lax.fori_loop(2 * quads, pairs, functools.partial(sum_step, 2), 0)
        numer = sum_ref[:HEAD_SIZE]
        top_ref[0, at : at + 1, :] = top
        total_ref[0, at : at + 1, :] = sum_ref[HEAD_SIZE : HEAD_SIZE + 1]
        for g in range(group):
            columns = slice(g * query_block, (g + 1) * query_block)
            out_columns = slice(g * HEAD_SIZE, (g + 1) * HEAD_SIZE)
            tokens = numer[:, columns].T
            if not rows_each:
                numer_refs[0][rows, out_columns] = tokens
                continue
            tokens = tokens.reshape(-1, CORES, rows_each, HEAD_SIZE)
            first = lax.rem(lax.axis_index("ctx"), CORES) == 0
            half = pl.ds(at * query_block // CORES, query_block // CORES)
            kept = jnp.where(first, tokens[:, 0], tokens[:, 1]).reshape(-1, HEAD_SIZE)
            sent = jnp.where(first, tokens[:, 1], tokens[:, 0]).reshape(-1, HEAD_SIZE)
            numer_refs[0][half, out_columns] = kept
            numer_refs[1][half, out_columns] = sent.astype(jnp.bfloat16)


def attend(whole, keys, values, block_mask, rows_each):
    qtok, width = whole.shape
    kdev = keys.shape[0]
    heads_kv, query_blocks, key_blocks = block_mask.shape
    columns = width // heads_kv
    lanes = columns // HEAD_SIZE * (qtok // query_blocks)
    stat = jax.ShapeDtypeStruct((heads_kv, query_blocks, lanes), jnp.float32)
    stat_spec = pl.BlockSpec((1, query_blocks, lanes), lambda h: (h, 0, 0))
    numers = [jax.ShapeDtypeStruct((qtok, width), jnp.float32)]
    if rows_each:
        numers = [jax.ShapeDtypeStruct((qtok // CORES, width), t) for t in (jnp.float32, jnp.bfloat16)]
    return pl.pallas_call(
        functools.partial(attend_kernel, rows_each),
        grid=(heads_kv,),
        out_shape=(*numers, stat, stat),
        in_specs=[
            pl.BlockSpec(memory_space=pltpu.SMEM),
            pl.BlockSpec((qtok, columns), lambda h: (0, h)),
            pl.BlockSpec((kdev, HEAD_SIZE), lambda h: (0, h)),
            pl.BlockSpec((kdev, HEAD_SIZE), lambda h: (0, h)),
        ],
        out_specs=(
            *(pl.BlockSpec((numer.shape[0], columns), lambda h: (0, h)) for numer in numers),
            stat_spec,
            stat_spec,
        ),
        scratch_shapes=[
            pltpu.SMEM((key_blocks + 2,), jnp.int32),
            pltpu.VMEM(((key_blocks + 1) // 2, 2 * kdev // key_blocks, lanes), jnp.float32),
            pltpu.VMEM((HEAD_SIZE, lanes), jnp.bfloat16),
            pltpu.VMEM((HEAD_SIZE + ONES, kdev), jnp.bfloat16),
            pltpu.VMEM((HEAD_SIZE + ONES, lanes), jnp.float32),
        ],
        compiler_params=pltpu.CompilerParams(vmem_limit_bytes=60 * 2**20),
        name="attend",
    )(block_mask, whole, keys, values)


def by_token(stat, qtok):
    heads_kv, query_blocks, _ = stat.shape
    stat = stat.reshape(heads_kv, query_blocks, -1, qtok // query_blocks)
    return stat.transpose(1, 3, 0, 2).reshape(qtok, -1)


def shards_any(queries, keys, values, block_mask, out_weight):
    whole = lax.all_gather(queries, "ctx", axis=0, tiled=True)
    qtok, width = whole.shape
    numer, top, total = attend(whole, keys, values, block_mask, 0)
    rescale = by_token(jnp.exp2(top - lax.pmax(top, "ctx")), qtok)
    denom = by_token(total, qtok) * rescale
    numer = (numer.reshape(qtok, -1, HEAD_SIZE) * rescale[:, :, None]).reshape(qtok, width)
    num_rows = lax.psum_scatter(numer, "ctx", scatter_dimension=0, tiled=True)
    den_rows = lax.psum_scatter(denom, "ctx", scatter_dimension=0, tiled=True)
    own_rows = num_rows.shape[0]
    attn_rows = (num_rows.reshape(own_rows, -1, HEAD_SIZE) / den_rows[:, :, None]).reshape(
        own_rows, width
    )
    attn_cols = lax.all_to_all(
        attn_rows.astype(jnp.bfloat16), "ctx", split_axis=1, concat_axis=0, tiled=True
    )
    summed = lax.psum_scatter(
        jnp.dot(attn_cols, out_weight, preferred_element_type=jnp.float32),
        "ctx",
        scatter_dimension=0,
        tiled=True,
    )
    return summed.astype(jnp.bfloat16)


def place(n):
    me = lax.axis_index("ctx")
    core = lax.rem(me, CORES)
    x = lax.rem(me // CORES, ROW)
    plane = me // (CORES * ROW)
    return me, plane, x, core


def index_of(plane, x, core):
    return (plane * ROW + x) * CORES + core


def remote(src, dst, send, recv, device):
    return pltpu.make_async_remote_copy(
        src_ref=src,
        dst_ref=dst,
        send_sem=send,
        recv_sem=recv,
        device_id={"ctx": device},
        device_id_type=MESH,
    )


LOW = -1e28
LANES = 128
SIDES = 2
TILE = 512


def swap_halves(stat):
    return pltpu.roll(stat, LANES // 2, 1)


def weigh(stats):
    lane = lax.broadcasted_iota(jnp.int32, stats[0].shape, 1)
    top = functools.reduce(jnp.maximum, stats)
    factors = [jnp.exp2(stat - top) for stat in stats]
    total = sum(stat * swap_halves(factor) for stat, factor in zip(stats, factors))
    return factors, jnp.where(lane < LANES // 2, top, total)


def column(tile, first, g, slots):
    lanes = [first + half * slots + g for half in range(2)]
    return jnp.concatenate([tile[:, lane : lane + 1] for lane in lanes], axis=0)


def layer_kernel(
    shape,
    own_hbm,
    k_hbm,
    v_hbm,
    mask_ref,
    w_hbm,
    out_ref,
    whole,
    k_ref,
    v_ref,
    w_ref,
    bias_ref,
    bias_out,
    score0,
    score1,
    top0,
    top1,
    local_sem,
    kv_sem,
    gather_sem,
    gather_plane_sem,
    beside_out,
    mine,
    beside_in,
    plane_out,
    own,
    plane_in,
    stat,
    stat_beside_in,
    stat_merged,
    stat_plane_in,
    sum_sem,
    sum_plane_sem,
    pieces,
    columns_ref,
    swap_sem,
    p_out,
    p_mine,
    p_in,
    p_plane_out,
    p_own,
    p_plane_in,
    p_last,
    p_sem,
    p_plane_sem,
):
    n, planes, heads, group, query_block, key_blocks, key_block = shape
    me, plane, x, core = place(n)
    beside, sibling = 1 - x, 1 - core
    rows = own_hbm.shape[0]
    span = planes // SIDES
    wide = group * HEAD_SIZE
    each = heads // CORES
    factor = LOG2E / math.sqrt(HEAD_SIZE)
    slots = 8
    pair, odd = plane // span, lax.rem(plane, span)
    near = pair * span + 1 - odd
    other = 1 - pair
    away = [other * span + odd, other * span + 1 - odd]
    others = [near] + away
    to_beside = index_of(plane, beside, core)
    to_sibling = index_of(plane, x, sibling)

    def lanes_at(start, width, unit=LANES):
        return pl.ds(pl.multiple_of(start, unit), width)

    def at_head(j):
        return lanes_at(j * wide, wide)

    half_width = each * wide
    queries_in = pltpu.make_async_copy(
        own_hbm.at[:, lanes_at(core * half_width, half_width)], whole.at[plane, x, core], local_sem.at[0]
    )
    queries_in.start()

    def kv_local(which, hbm, ref, j):
        return pltpu.make_async_copy(
            hbm.at[:, lanes_at((core * each + j) * HEAD_SIZE, HEAD_SIZE)],
            ref.at[core, :, lanes_at(j * HEAD_SIZE, HEAD_SIZE)],
            kv_sem.at[which, j],
        )

    def kv_remote(which, hbm, ref, j, source):
        return remote(
            hbm.at[:, lanes_at((sibling * each + j) * HEAD_SIZE, HEAD_SIZE)],
            ref.at[source, :, lanes_at(j * HEAD_SIZE, HEAD_SIZE)],
            kv_sem.at[2 + which, j],
            kv_sem.at[4 + which, j],
            to_sibling,
        )

    kv = [(0, k_hbm, k_ref), (1, v_hbm, v_ref)]
    w_local = pltpu.make_async_copy(
        w_hbm.at[:, lanes_at(core * half_width, half_width)], w_ref.at[core], local_sem.at[1]
    )

    def w_remote(source):
        return remote(
            w_hbm.at[:, lanes_at(sibling * half_width, half_width)],
            w_ref.at[source],
            local_sem.at[2],
            local_sem.at[3],
            to_sibling,
        )

    def queries_remote(source):
        return remote(
            own_hbm.at[:, lanes_at(sibling * half_width, half_width)],
            whole.at[plane, x, source],
            local_sem.at[4],
            local_sem.at[5],
            to_sibling,
        )

    def bias_remote(source):
        return remote(bias_out, bias_ref.at[source], local_sem.at[6], local_sem.at[7], to_sibling)

    for which, hbm, ref in kv:
        kv_local(which, hbm, ref, 0).start()
    barrier = pltpu.get_barrier_semaphore()
    greeted = [to_sibling, to_beside] + [index_of(p, x, core) for p in others]
    for device in greeted:
        pl.semaphore_signal(barrier, inc=1, device_id={"ctx": device}, device_id_type=MESH)

    def bias_step(row, _):
        j, t, b = row // (SIDES * key_blocks), row // key_blocks % SIDES, row % key_blocks
        for which, ref in ((core, bias_ref.at[core]), (sibling, bias_out)):
            value = jnp.where(mask_ref[which * each + j, t, b] > 0, 0.0, NEG)
            ref[pl.ds(row, 1), :] = jnp.full((1, LANES), value, jnp.float32)
        return 0

    lax.fori_loop(0, each * SIDES * key_blocks, bias_step, 0)
    pl.semaphore_wait(barrier, len(greeted))
    queries_remote(core).start()
    bias_remote(core).start()
    for which, hbm, ref in kv:
        kv_remote(which, hbm, ref, 0, core).start()

    def gather_plane(j, p, source):
        block = whole.at[source, x, :, :, at_head(j)]
        return remote(
            block,
            block,
            gather_plane_sem.at[0, j, p],
            gather_plane_sem.at[1, j, source],
            index_of(p, x, core),
        )

    def gather_beside(j, t, side):
        block = whole.at[pl.ds(t * span, span), side, :, :, at_head(j)]
        return remote(block, block, gather_sem.at[0, j, t], gather_sem.at[1, j, t], to_beside)

    def gather0(j):
        for p in others:
            gather_plane(j, p, plane).start()

    def gather1(j, t):
        for p in [near] if t is pair else away:
            gather_plane(j, p, p).wait_recv()
        gather_beside(j, t, x).start()

    def gather2(j, t):
        gather_beside(j, t, beside).wait_recv()

    def kv_start(j):
        for which, hbm, ref in kv:
            kv_local(which, hbm, ref, j).start()
            kv_remote(which, hbm, ref, j, core).start()

    def kv_ready(j):
        for which, hbm, ref in kv:
            kv_local(which, hbm, ref, j).wait()
            kv_remote(which, hbm, ref, j, sibling).wait_recv()

    pairs = key_blocks // 2

    def score_item(j, t, score, top_ref):
        tokens = whole.at[pl.ds(t * span, span)]
        query = jnp.concatenate(
            [
                tokens[:, :, :, :, lanes_at(j * wide + g * HEAD_SIZE, HEAD_SIZE)].reshape(
                    query_block, HEAD_SIZE
                )
                for g in range(group)
            ],
            axis=0,
        )
        top = None
        first_row = (j * SIDES + t) * key_blocks
        for which in range(CORES):
            for two in range(pairs):
                at = slice(2 * two * key_block, 2 * (two + 1) * key_block)
                scores = lax.dot_general(
                    query,
                    k_ref[which, at, lanes_at(j * HEAD_SIZE, HEAD_SIZE)],
                    (((1,), (1,)), ((), ())),
                    preferred_element_type=jnp.float32,
                )
                for b in range(2):
                    block = 2 * two + b
                    bias = bias_ref[which, pl.ds(first_row + block, 1), :]
                    part = scores[:, b * key_block : (b + 1) * key_block] + bias
                    to = (which * key_blocks + block) * key_block
                    score[:, to : to + key_block] = part
                    top = part if top is None else jnp.maximum(top, part)
        top = jnp.maximum(jnp.max(top, axis=1, keepdims=True) * factor, LOW)
        top_ref[...] = jnp.broadcast_to(top, top_ref.shape)

    def sum_item(j, t, score, top_ref):
        top = top_ref[...]
        shift = jnp.concatenate([top, top], axis=1)
        both = None
        for which in range(CORES):
            for two in range(pairs):
                at = slice(2 * two * key_block, 2 * (two + 1) * key_block)
                to = (which * key_blocks + 2 * two) * key_block
                probs = jnp.exp2(score[:, to : to + 2 * key_block] * factor - shift).astype(jnp.bfloat16)
                values = jnp.concatenate(
                    [
                        v_ref[which, at, lanes_at(j * HEAD_SIZE, HEAD_SIZE)],
                        jnp.ones((2 * key_block, HEAD_SIZE), jnp.bfloat16),
                    ],
                    axis=1,
                )
                part = jnp.dot(probs, values, preferred_element_type=jnp.float32)
                both = part if both is None else both + part
        split = (group, span, ROW, CORES, rows, HEAD_SIZE)
        numer = both[:, :HEAD_SIZE].reshape(split)
        total = both[:, HEAD_SIZE:].reshape(split)
        tops = top.reshape(split)
        for g in range(group):
            at = slice(g * HEAD_SIZE, (g + 1) * HEAD_SIZE)
            one, two = numer[g, :, 0], numer[g, :, 1]
            mine[j, t, :, :, :, at] = jnp.where(x == 0, one, two)
            beside_out[j, t, :, :, :, at] = jnp.where(x == 0, two, one).astype(jnp.bfloat16)
        lane = lax.broadcasted_iota(jnp.int32, (8, LANES), 1)
        for side in range(ROW):
            tile = jnp.zeros((8, LANES), jnp.float32)
            for q in range(span):
                for which in range(CORES):
                    for half in range(rows // 8):
                        at = slice(half * 8, half * 8 + 8)
                        for g in range(group):
                            to = ((q * CORES + which) * 2 + half) * slots + g
                            tile = jnp.where(lane == to, tops[g, q, side, which, at], tile)
                            to = to + LANES // 2
                            tile = jnp.where(lane == to, total[g, q, side, which, at], tile)
            stat[j, t, side] = tile

    def to_side(j, t):
        return [
            remote(
                beside_out.at[j, t],
                beside_in.at[j, t],
                sum_sem.at[0, j, t],
                sum_sem.at[1, j, t],
                to_beside,
            ),
            remote(
                stat.at[j, t, beside],
                stat_beside_in.at[j, t],
                sum_sem.at[2, j, t],
                sum_sem.at[3, j, t],
                to_beside,
            ),
        ]

    def to_plane(j, t, p, slot):
        device = index_of(p, x, core)
        return [
            remote(
                plane_out.at[j, p],
                plane_in.at[j, slot],
                sum_plane_sem.at[0, j, p],
                sum_plane_sem.at[1, j, slot],
                device,
            ),
            remote(
                stat_merged.at[j, t],
                stat_plane_in.at[j, slot],
                sum_plane_sem.at[2, j, p],
                sum_plane_sem.at[3, j, slot],
                device,
            ),
        ]

    def start(copies):
        for copy in copies:
            copy.start()

    def arrive(copies):
        for copy in copies:
            copy.wait_recv()

    def leave(copies):
        for copy in copies:
            copy.wait_send()

    def sum0(j, t):
        start(to_side(j, t))

    def sum1(j, t):
        arrive(to_side(j, t))
        factors, merged = weigh([stat[j, t, x], stat_beside_in[j, t]])
        stat_merged[j, t] = merged
        for q in range(span):
            values = []
            for which in range(CORES):
                first = (q * CORES + which) * 2 * slots
                parts = []
                for g in range(group):
                    at = slice(g * HEAD_SIZE, (g + 1) * HEAD_SIZE)
                    one, two = [column(tile, first, g, slots) for tile in factors]
                    parts.append(
                        mine[j, t, q, which, :, at] * one
                        + beside_in[j, t, q, which, :, at].astype(jnp.float32) * two
                    )
                values.append(jnp.concatenate(parts, axis=1))
            p = t * span + q

            def keep():
                for which in range(CORES):
                    own[j, which] = values[which]

            def send():
                for which in range(CORES):
                    plane_out[j, p, which] = values[which].astype(jnp.bfloat16)
                start(to_plane(j, t, p, plane))

            if t is pair:
                pl.when(plane == p)(keep)
                pl.when(plane != p)(send)
            else:
                send()

    def swap(j, which, slot):
        head = core * each + j
        device = index_of(head // ROW, head % ROW, 1 - which)
        return remote(
            pieces.at[j, which],
            columns_ref.at[slot // ROW, slot % ROW, which],
            swap_sem.at[0, j, which],
            swap_sem.at[1, 0, slot],
            device,
        )

    def keep_piece(j):
        return pltpu.make_async_copy(
            pieces.at[j, sibling], columns_ref.at[plane, x, sibling], local_sem.at[8]
        )

    def columns_on(which):
        block = columns_ref.at[:, :, which]
        return remote(block, block, local_sem.at[9], local_sem.at[10], to_sibling)

    slot = plane * ROW + x

    def owner(j, which):
        head = core * each + j
        return index_of(head // ROW, head % ROW, 1 - which)

    def sum2(j):
        for p in others:
            arrive(to_plane(j, 0, p, p))
        tiles = [stat_merged[j, pair]] + [stat_plane_in[j, p] for p in others]
        tiles = [jnp.where(odd == 1, swap_quarter(tile), tile) for tile in tiles]
        factors, merged = weigh(tiles)
        merged = swap_halves(merged)
        for which in range(CORES):
            first = which * 2 * slots
            for g in range(group):
                at = slice(g * HEAD_SIZE, (g + 1) * HEAD_SIZE)
                value = own[j, which, :, at] * column(factors[0], first, g, slots)
                for p, one in zip(others, factors[1:]):
                    value = value + plane_in[j, p, which, :, at].astype(jnp.float32) * column(
                        one, first, g, slots
                    )
                value = value / column(merged, first, g, slots)
                pieces[j, which, :, at] = value.astype(jnp.bfloat16)
        for which in range(CORES):

            @pl.when(owner(j, which) == me)
            def _():
                keep_piece(j).start()

            @pl.when(owner(j, which) != me)
            def _():
                swap(j, which, slot).start()

    def swap_quarter(tile):
        return pltpu.roll(tile, LANES - 4 * slots, 1)

    def on(cond, act):
        pl.when(cond)(act)

    queries_in.wait()
    queries_remote(sibling).wait_recv()
    gather0(0)
    gather1(0, pair)
    gather0(1)
    kv_start(1)
    gather1(0, other)
    gather0(2)
    gather1(1, pair)
    bias_remote(sibling).wait_recv()
    kv_ready(0)
    gather2(0, pair)
    score_item(0, pair, score0, top0)

    def head_step(final, j, _):
        on(j >= 1, lambda: sum0(j - 1, other))
        on(j + 3 < each, lambda: gather0(j + 3))
        on(j + 2 < each, lambda: kv_start(j + 2))
        on(j + 1 < each, lambda: gather1(j + 1, other))
        gather2(j, other)
        on(j >= 2, lambda: sum1(j - 2, other))
        score_item(j, other, score1, top1)
        sum_item(j, pair, score0, top0)
        sum0(j, pair)
        on(j + 2 < each, lambda: gather1(j + 2, pair))

        @pl.when(j + 1 < each)
        def _():
            kv_ready(j + 1)
            gather2(j + 1, pair)

        on(j >= 1, lambda: sum1(j - 1, pair))

        @pl.when(j == 1)
        def _():
            w_local.start()
            w_remote(core).start()

        if not final:
            score_item(j + 1, pair, score0, top0)
        sum_item(j, other, score1, top1)
        return 0

    lax.fori_loop(0, each - 1, functools.partial(head_step, False), 0)
    lax.fori_loop(each - 1, each, functools.partial(head_step, True), 0)
    last = each - 1
    for act, *which in (
        (sum0, last, other),
        (sum1, last - 1, other),
        (sum2, 0),
        (sum1, last, pair),
        (sum2, last - 2),
        (sum1, last, other),
        (sum2, last - 1),
        (sum2, last),
    ):
        act(*which)
    w_local.wait()
    w_remote(sibling).wait_recv()

    def take_piece(at, _):
        on(jnp.logical_or(core != pair, at != slot), lambda: swap(0, sibling, at).wait_recv())
        return 0

    lax.fori_loop(0, planes * ROW, take_piece, 0)
    on(core == pair, lambda: keep_piece(0).wait())
    columns_on(sibling).start()

    tiles = half_width // TILE
    units = 2 * tiles

    def p_side(u):
        return remote(p_out.at[u], p_in.at[u], p_sem.at[0, u], p_sem.at[1, u], to_beside)

    def p_plane(u, p, slot):
        return remote(
            p_plane_out.at[u, p],
            p_plane_in.at[u, slot],
            p_plane_sem.at[0, u, p],
            p_plane_sem.at[1, u, slot],
            index_of(p, x, core),
        )

    def out_at(side, c):
        return out_ref.at[:, lanes_at(side * half_width + c * TILE, TILE)]

    def p_end(c, side):
        return remote(p_last.at[c], out_at(side, c), p_sem.at[2, c], p_sem.at[3, c], to_sibling)

    def project0(c, which, u):
        cols = columns_ref[:, :, which].reshape(planes * ROW * rows, wide)
        weight = w_ref[:, :, lanes_at(c * TILE, TILE)].reshape(wide, TILE)
        product = jnp.dot(cols, weight, preferred_element_type=jnp.float32)
        product = product.reshape(planes, ROW, rows, TILE)
        one, two = product[:, 0], product[:, 1]
        p_out[u] = jnp.where(x == 0, two, one).astype(jnp.bfloat16)
        p_side(u).start()
        p_mine[u] = jnp.where(x == 0, one, two)

    def project1(u):
        p_side(u).wait_recv()
        for p in others:
            value = p_mine[u, p] + p_in[u, p].astype(jnp.float32)
            p_plane_out[u, p] = value.astype(jnp.bfloat16)
            p_plane(u, p, plane).start()
        p_own[u] = p_mine[u, plane] + p_in[u, plane].astype(jnp.float32)

    def project2(u):
        value = p_own[u]
        for p in others:
            p_plane(u, p, p).wait_recv()
        for p in others:
            value = value + p_plane_in[u, p].astype(jnp.float32)
        return value.astype(jnp.bfloat16)

    def loop(count, act):
        def step(c, _):
            act(c)
            return 0

        lax.fori_loop(0, count, step, 0)

    def finish_sibling(c):
        p_last[c] = project2(c)
        p_end(c, core).start()

    def finish_own(c):
        out_ref[:, lanes_at(core * half_width + c * TILE, TILE)] = project2(tiles + c)

    loop(tiles, lambda c: project0(c, sibling, c))
    columns_on(core).wait_recv()
    loop(tiles, lambda c: project0(c, core, tiles + c))
    loop(units, project1)
    loop(tiles, finish_sibling)
    loop(tiles, finish_own)

    def p_drain(c):
        p_end(c, sibling).wait_recv()
        p_end(c, core).wait_send()

    def u_drain(u):
        p_side(u).wait_send()
        for p in others:
            p_plane(u, p, plane).wait_send()

    loop(tiles, p_drain)
    loop(units, u_drain)
    columns_on(sibling).wait_send()

    def drain(j):
        for p in others:
            gather_plane(j, p, plane).wait_send()
        for t in range(SIDES):
            gather_beside(j, t, x).wait_send()
            leave(to_side(j, t))
        for which, hbm, ref in kv:
            kv_remote(which, hbm, ref, j, core).wait_send()
        for p in others:
            leave(to_plane(j, 0, p, plane))
        for which in range(CORES):
            on(owner(j, which) != me, lambda: swap(j, which, slot).wait_send())

    loop(each, drain)
    queries_remote(core).wait_send()
    bias_remote(core).wait_send()
    w_remote(core).wait_send()


def layer(queries, keys, values, block_mask, weight, n):
    rows, width = queries.shape
    heads, query_blocks, key_blocks = block_mask.shape
    kdev = keys.shape[0]
    planes = n // (CORES * ROW)
    wide = width // heads
    group = wide // HEAD_SIZE
    query_block = n * rows // query_blocks
    span = planes // query_blocks
    each = heads // CORES
    tiles = width // CORES // TILE
    items = (each, query_blocks)
    bf16, f32 = jnp.bfloat16, jnp.float32
    dma = pltpu.SemaphoreType.DMA
    lanes = group * query_block
    shape = (n, planes, heads, group, query_block, key_blocks, kdev // key_blocks)
    tile = (rows, TILE)
    units = CORES * tiles
    block = (CORES, rows, wide)
    return pl.pallas_call(
        functools.partial(layer_kernel, shape),
        out_shape=jax.ShapeDtypeStruct((rows, width), bf16),
        in_specs=[
            pl.BlockSpec(memory_space=pl.ANY),
            pl.BlockSpec(memory_space=pl.ANY),
            pl.BlockSpec(memory_space=pl.ANY),
            pl.BlockSpec(memory_space=pltpu.SMEM),
            pl.BlockSpec(memory_space=pl.ANY),
        ],
        out_specs=pl.BlockSpec(memory_space=pltpu.VMEM),
        scratch_shapes=[
            pltpu.VMEM((planes, ROW, CORES, rows, width // CORES), bf16),
            pltpu.VMEM((CORES, kdev, each * HEAD_SIZE), bf16),
            pltpu.VMEM((CORES, kdev, each * HEAD_SIZE), bf16),
            pltpu.VMEM((CORES, weight.shape[0], width // CORES), bf16),
            pltpu.VMEM((CORES, each * query_blocks * key_blocks, LANES), f32),
            pltpu.VMEM((each * query_blocks * key_blocks, LANES), f32),
            pltpu.VMEM((lanes, CORES * kdev), f32),
            pltpu.VMEM((lanes, CORES * kdev), f32),
            pltpu.VMEM((lanes, LANES), f32),
            pltpu.VMEM((lanes, LANES), f32),
            dma((11,)),
            dma((6, each)),
            dma((2, *items)),
            dma((2, each, planes)),
            pltpu.VMEM((*items, span, *block), bf16),
            pltpu.VMEM((*items, span, *block), f32),
            pltpu.VMEM((*items, span, *block), bf16),
            pltpu.VMEM((each, planes, *block), bf16),
            pltpu.VMEM((each, *block), f32),
            pltpu.VMEM((each, planes, *block), bf16),
            pltpu.VMEM((*items, ROW, 8, LANES), f32),
            pltpu.VMEM((*items, 8, LANES), f32),
            pltpu.VMEM((*items, 8, LANES), f32),
            pltpu.VMEM((each, planes, 8, LANES), f32),
            dma((4, *items)),
            dma((4, each, planes)),
            pltpu.VMEM((each, *block), bf16),
            pltpu.VMEM((planes, ROW, *block), bf16),
            dma((2, each, planes * ROW)),
            pltpu.VMEM((units, planes, *tile), bf16),
            pltpu.VMEM((units, planes, *tile), f32),
            pltpu.VMEM((units, planes, *tile), bf16),
            pltpu.VMEM((units, planes, *tile), bf16),
            pltpu.VMEM((units, *tile), f32),
            pltpu.VMEM((units, planes, *tile), bf16),
            pltpu.VMEM((tiles, *tile), bf16),
            dma((4, units)),
            dma((2, units, planes)),
        ],
        compiler_params=pltpu.CompilerParams(
            collective_id=0, has_side_effects=True, vmem_limit_bytes=60 * 2**20
        ),
        name="layer",
    )(queries, keys, values, block_mask, weight)


def solution(mesh):
    n = mesh.shape["ctx"]

    def shards(queries, keys, values, block_mask, out_weight):
        rows, width = queries.shape
        heads, query_blocks, key_blocks = block_mask.shape
        planes = n // (CORES * ROW)
        group = width // heads // HEAD_SIZE
        fits = (
            n == CORES * ROW * planes
            and n == 2 * heads
            and rows == 16
            and query_blocks == SIDES
            and planes == 2 * SIDES
            and group <= 8
            and key_blocks % 2 == 0
            and width % (CORES * TILE) == 0
        )
        if fits:
            return layer(queries, keys, values, block_mask, out_weight, n)
        return shards_any(queries, keys, values, block_mask, out_weight)

    return jax.shard_map(
        shards,
        mesh=mesh,
        in_specs=(
            P(("groups", "ctx"), None),
            P(("groups", "ctx"), None),
            P(("groups", "ctx"), None),
            P("groups", None, "ctx"),
            P("ctx", None),
        ),
        out_specs=P(("groups", "ctx"), None),
        check_vma=False,
    )
```
